32 devices in a mesh: rows: 8 (over z, y), band: 4 (over x, core).
Axes of the slice: x: 2, y: 2, z: 4, core: 2. Of those that a mesh axis runs over, the one named last changes fastest.
Arguments:
- embedding: bfloat16 [1024, 512], P('rows'), may hold values from -6 to 6
- w_left: bfloat16 [512, 32], replicated, may hold values from -0.25 to 0.25
- w_right: bfloat16 [512, 32], replicated, may hold values from -0.25 to 0.25
- w_in: bfloat16 [32, 128], replicated, may hold values from -1 to 1
- w_out: bfloat16 [128, 32], replicated, may hold values from -0.5 to 0.5
- w_head: float32 [32], replicated, may hold values from -1 to 1
- dist_bias: float32 [32, 4], replicated, may hold values from -3 to 3
- offsets: int32 [8, 4], P('rows', 'band'), may hold values from 0 to 3, each once within a row
- valid_bins: int32 [1024], P('rows'), may hold values 0 or 1
- target: bfloat16 [8, 4, 128, 128], P('rows', 'band'), may hold values from -6 to 6
Outputs:
- predicted: bfloat16 [8, 4, 128, 128], P('rows', 'band')
- grad_embedding: bfloat16 [1024, 512], P('rows', 'band')
- grad_left: float32 [512, 32], replicated
- grad_right: float32 [512, 32], replicated
- grad_in: float32 [32, 128], replicated
- grad_out: float32 [128, 32], replicated
- grad_head: float32 [32], replicated
- grad_bias: float32 [32, 4], replicated
The draws below stay inside these ranges and needn't reach their ends.
Inputs may be any that keep to these rules, and one draw needn't show every extreme that they name: `offsets`: each row tile's 4 entries are the numbers 0 to 3 in some order.
All inputs are finite; a program needn't handle non-finite values. No bound on the sum of `valid_bins` on one device may be relied on, other than what follows from the above.
Results may differ from the reference program's by a relative error of at most 0.0058.
Values may be sent and summed in bfloat16 or wider, within the bound.
No kernel may reach another device: no remote copies, remote signals or barrier semaphores. Data moves between devices by JAX's collectives and lax.ppermute only.
A program may use at most 64 MiB of HBM per device.

```python
import jax
import jax.numpy as jnp
from jax import lax

C = 512
P_SIZE = 32
HID = 128
TILE = 128
NOFF = 4
ROW_TILES = 8
BINS = 1024


def with_ends(array, own_key, smallest, top_value):
    index_at = [jax.random.randint(jax.random.fold_in(own_key, axis), (), 0, length) for axis, length in enumerate(array.shape)]
    main_axis = array.shape.index(max(array.shape))
    next_to = index_at[:main_axis] + [(index_at[main_axis] + 1) % array.shape[main_axis]] + index_at[main_axis + 1:]
    return array.at[tuple(index_at)].set(smallest).at[tuple(next_to)].set(top_value)


def block_scale(own_key, shape, pieces, least, largest):
    level, own = 1.0, jax.random.fold_in(own_key, 6)
    for axis_at, shards_of in pieces:
        heights = jnp.exp(jax.random.uniform(jax.random.fold_in(own, axis_at), (shards_of,), jnp.float32, least / len(pieces), largest / len(pieces)))
        level = level * jnp.repeat(heights, shape[axis_at] // shards_of).reshape([-1 if axis == axis_at else 1 for axis in range(len(shape))])
    return level


def gaussian(own_key, shape, width, most, split=(), held_as=jnp.bfloat16):
    drawn = width * jax.random.normal(own_key, shape, jnp.float32)
    if split:
        drawn = drawn * block_scale(own_key, shape, split, -0.22, 0.18)
    return jnp.clip(drawn, -most, most).astype(held_as)


def setup_inputs(seed: int = 0) -> dict:
    key_list = jax.random.split(jax.random.key(seed), 11)
    return {
        "embedding": gaussian(key_list[0], (BINS, C), 1.0, 6.0, ((0, 8),)),
        "w_left": gaussian(key_list[1], (C, P_SIZE), C ** -0.5, 0.25),
        "w_right": gaussian(key_list[2], (C, P_SIZE), C ** -0.5, 0.25),
        "w_in": gaussian(key_list[3], (P_SIZE, HID), P_SIZE ** -0.5, 1.0),
        "w_out": gaussian(key_list[4], (HID, P_SIZE), HID ** -0.5, 0.5),
        "w_head": gaussian(key_list[5], (P_SIZE,), P_SIZE ** -0.5, 1.0, (), jnp.float32),
        "dist_bias": gaussian(key_list[6], (P_SIZE, NOFF), 0.5, 3.0, (), jnp.float32),
        "offsets": jax.vmap(lambda own: jax.random.permutation(own, NOFF))(jax.random.split(key_list[7], ROW_TILES)).reshape((ROW_TILES, NOFF)).astype(jnp.int32),
        "valid_bins": with_ends((jax.random.randint(key_list[8], (BINS,), 0, 8) < 7).astype(jnp.int32), jax.random.fold_in(key_list[8], 1), 0, 1),
        "target": gaussian(key_list[9], (ROW_TILES, NOFF, TILE, TILE), 1.0, 6.0, ((0, 8), (1, 4))),
    }


def gelu_pair(pre_act):
    return jax.nn.gelu(pre_act, approximate=True)

def block_terms(row_proj, col_proj, bias_col, row_flags, col_flags, goal_rows, w_in, w_out, w_head):
    channels = row_proj.shape[0]
    row_count = row_proj.shape[1]
    col_count = col_proj.shape[1]
    summed = row_proj.astype(jnp.float32)[:, :, None] + col_proj.astype(jnp.float32)[:, None, :] + bias_col[:, None, None]
    summed = summed.reshape(channels, row_count * col_count)
    pair_in = summed.astype(jnp.bfloat16)
    pre_act = lax.dot_general(w_in, pair_in, (((0,), (0,)), ((), ())), preferred_element_type=jnp.float32)
    activation = gelu_pair(pre_act).astype(jnp.bfloat16)
    update = summed + lax.dot_general(w_out, activation, (((0,), (0,)), ((), ())), preferred_element_type=jnp.float32)
    logits = jnp.dot(w_head, update, precision=lax.Precision.HIGHEST)
    weight_mask = (row_flags[:, None] * col_flags[None, :]).reshape(-1)
    residual = weight_mask * (logits - goal_rows.astype(jnp.float32).reshape(-1)) / (NOFF * TILE)
    grad_update = w_head[:, None] * residual[None, :]
    grad_low = grad_update.astype(jnp.bfloat16)
    head_term = jnp.dot(update, residual, precision=lax.Precision.HIGHEST)
    out_term = lax.dot_general(activation, grad_low, (((1,), (1,)), ((), ())), preferred_element_type=jnp.float32)
    grad_act = lax.dot_general(w_out, grad_low, (((1,), (0,)), ((), ())), preferred_element_type=jnp.float32)
    _, backward = jax.vjp(gelu_pair, pre_act)
    grad_pre = backward(grad_act)[0].astype(jnp.bfloat16)
    in_term = lax.dot_general(pair_in, grad_pre, (((1,), (1,)), ((), ())), preferred_element_type=jnp.float32)
    grad_pair = grad_update + lax.dot_general(w_in, grad_pre, (((1,), (0,)), ((), ())), preferred_element_type=jnp.float32)
    grad_cube = grad_pair.reshape(channels, row_count, col_count)
    return (logits.reshape(row_count, col_count), head_term, out_term, in_term, lax.optimization_barrier(jnp.sum(grad_pair, axis=1)), lax.optimization_barrier(jnp.sum(grad_cube, axis=2)), lax.optimization_barrier(jnp.sum(grad_cube, axis=1)))

def tile_terms(row_proj, col_proj, bias_col, row_flags, col_flags, goal_tile, w_in, w_out, w_head):
    half_rows = row_proj.shape[1] // 2
    first = block_terms(row_proj[:, :half_rows], col_proj, bias_col, row_flags[:half_rows], col_flags, goal_tile[:half_rows], w_in, w_out, w_head)
    second = block_terms(row_proj[:, half_rows:], col_proj, bias_col, row_flags[half_rows:], col_flags, goal_tile[half_rows:], w_in, w_out, w_head)
    return (jnp.concatenate([first[0], second[0]], axis=0), first[1] + second[1], first[2] + second[2], first[3] + second[3], first[4] + second[4], jnp.concatenate([first[5], second[5]], axis=1), first[6] + second[6])

def project(embedding, weight):
    return lax.dot_general(weight, embedding, (((0,), (1,)), ((), ())), preferred_element_type=jnp.float32).astype(jnp.bfloat16)

def reference(embedding, w_left, w_right, w_in, w_out, w_head, dist_bias, offsets, valid_bins, target):
    left_proj = project(embedding, w_left)
    right_proj = project(embedding, w_right)
    margin = NOFF * TILE
    right_pad = jnp.pad(right_proj, ((0, 0), (0, margin)))
    flags_pad = jnp.pad(valid_bins.astype(jnp.float32), (0, margin))
    channels = w_left.shape[1]
    hidden = w_in.shape[1]
    initial = (jnp.zeros((channels, BINS), jnp.float32), jnp.zeros((channels, BINS + margin), jnp.float32), jnp.zeros((channels, hidden), jnp.float32), jnp.zeros((hidden, channels), jnp.float32), jnp.zeros((channels,), jnp.float32), jnp.zeros((channels, NOFF), jnp.float32))

    def advance(totals, item_index):
        tile_row = item_index // NOFF
        slot_index = item_index % NOFF
        offset = offsets[tile_row, slot_index]
        one_hot = (jnp.arange(NOFF, dtype=jnp.int32) == offset).astype(jnp.float32)
        bias_col = lax.optimization_barrier(jnp.sum(dist_bias * one_hot[None, :], axis=1))
        row_start = (tile_row * TILE).astype(jnp.int32)
        col_start = ((tile_row + offset) * TILE).astype(jnp.int32)
        row_proj = lax.dynamic_slice_in_dim(left_proj, row_start, TILE, 1)
        col_proj = lax.dynamic_slice_in_dim(right_pad, col_start, TILE, 1)
        row_flags = lax.dynamic_slice_in_dim(flags_pad, row_start, TILE, 0)
        col_flags = lax.dynamic_slice_in_dim(flags_pad, col_start, TILE, 0)
        goal_tile = target[tile_row, slot_index]
        logits, head_term, out_term, in_term, bias_sum, row_sums, col_sums = tile_terms(row_proj, col_proj, bias_col, row_flags, col_flags, goal_tile, w_in, w_out, w_head)
        row_acc, col_acc, in_acc, out_acc, head_acc, bias_acc = totals
        row_acc = lax.dynamic_update_slice_in_dim(row_acc, lax.dynamic_slice_in_dim(row_acc, row_start, TILE, 1) + row_sums, row_start, 1)
        col_acc = lax.dynamic_update_slice_in_dim(col_acc, lax.dynamic_slice_in_dim(col_acc, col_start, TILE, 1) + col_sums, col_start, 1)
        bias_acc = bias_acc + bias_sum[:, None] * one_hot[None, :]
        return ((row_acc, col_acc, in_acc + in_term, out_acc + out_term, head_acc + head_term, bias_acc), logits)
    totals, logits = lax.scan(advance, initial, jnp.arange(ROW_TILES * NOFF, dtype=jnp.int32))
    row_acc, col_acc, grad_in, grad_out, grad_head, grad_bias = totals
    predicted = logits.reshape(ROW_TILES, NOFF, TILE, TILE).astype(jnp.bfloat16)
    row_grad = row_acc.astype(jnp.bfloat16)
    col_grad = col_acc[:, :BINS].astype(jnp.bfloat16)
    grad_embedding = (lax.dot_general(row_grad, w_left, (((0,), (1,)), ((), ())), preferred_element_type=jnp.float32) + lax.dot_general(col_grad, w_right, (((0,), (1,)), ((), ())), preferred_element_type=jnp.float32)).astype(jnp.bfloat16)
    grad_left = lax.dot_general(embedding, row_grad, (((0,), (1,)), ((), ())), preferred_element_type=jnp.float32)
    grad_right = lax.dot_general(embedding, col_grad, (((0,), (1,)), ((), ())), preferred_element_type=jnp.float32)
    return (predicted, grad_embedding, grad_left, grad_right, grad_in, grad_out, grad_head, grad_bias)
```

```python
import math

import jax
import jax.numpy as jnp
from jax import lax
from jax.experimental import pallas as pl
from jax.experimental.pallas import tpu as pltpu
from jax.sharding import PartitionSpec as P

BF = jnp.bfloat16
F32 = jnp.float32
CURVE = math.sqrt(2.0 / math.pi)
CUBIC = 0.044715 * CURVE
GROUP = 8
HALVES = 2
NT = (((1,), (1,)), ((), ()))
NN = (((1,), (0,)), ((), ()))


def mm(a, b, dims=NN):
    return lax.dot_general(a, b, dims, preferred_element_type=F32)


def split(x):
    high = x.astype(BF)
    return high, (x - high.astype(F32)).astype(BF)


def mm_wide(a, b, dims=NN):
    high, low = split(b)
    return mm(a, high, dims) + mm(a, low, dims)


def eye(count):
    return lax.broadcasted_iota(jnp.int32, (count, count), 0) == lax.broadcasted_iota(
        jnp.int32, (count, count), 1
    )


def to_col(row):
    count = row.shape[1]
    return jnp.sum(jnp.where(eye(count), jnp.broadcast_to(row, (count, count)), 0.0), axis=1, keepdims=True)


def to_row(col):
    count = col.shape[0]
    return jnp.sum(jnp.where(eye(count), jnp.broadcast_to(col, (count, count)), 0.0), axis=0, keepdims=True)


def project_kernel(emb_ref, wl_ref, wr_ref, flags_ref, left_ref, send_ref):
    channels = wl_ref.shape[1]
    emb = emb_ref[...]
    bins = emb.shape[0]
    pad = jnp.zeros((bins, bins - 2 * channels), F32)
    both = jnp.concatenate([mm(emb, wl_ref[...]), mm(emb, wr_ref[...]), pad], axis=1).T
    left_ref[...] = both[:channels].astype(BF)
    flags = jnp.broadcast_to(flags_ref[...].astype(F32), (GROUP, bins))
    piece = jnp.concatenate([both[channels : 2 * channels], flags], axis=0).astype(BF)
    for row in range(send_ref.shape[0]):
        send_ref[row] = piece


def tile_kernel(
    info_ref,
    left_ref,
    recv_ref,
    flags_ref,
    target_ref,
    w_in_ref,
    w_out_ref,
    w_head_ref,
    bias_ref,
    pred_ref,
    send_ref,
    target_wide,
    act_ref,
    slope_ref,
    logit_ref,
    res_ref,
    row_ref,
    col_ref,
    act_sum_ref,
    logit_col_ref,
    flag_col_ref,
):
    channels, hidden = w_in_ref.shape
    tile = target_ref.shape[0]
    noff = bias_ref.shape[1]
    rows = recv_ref.shape[0]
    bands = send_ref.shape[0] // rows
    part = 2 * channels // bands
    here, offset = info_ref[0], info_ref[1]
    there = here + offset
    inside = (there < rows).astype(F32)
    piece = recv_ref[jnp.minimum(there, rows - 1)].astype(F32) * inside
    right = piece[:channels]
    col_flags = piece[channels : channels + 1] * (1.0 / (noff * tile))
    left = left_ref[...].astype(F32)
    lane_off = lax.broadcasted_iota(jnp.int32, (channels, noff), 1)
    bias = jnp.sum(jnp.where(lane_off == offset, bias_ref[...], 0.0), axis=1, keepdims=True)
    head_row = w_head_ref[...]
    head = to_col(head_row)
    gain = jnp.sum(w_out_ref[...].astype(F32) * head_row, axis=1, keepdims=True) * 0.5
    gain_row = to_row(gain)
    logit_col_ref[...] = to_col(jnp.sum((left + bias) * head, axis=0, keepdims=True))
    logit_row = jnp.sum(right * head, axis=0, keepdims=True)
    flag_col_ref[...] = to_col(flags_ref[...].astype(F32))
    target_wide[...] = target_ref[...].astype(F32)
    shifted = right + bias
    w_in = w_in_ref[...]
    w_in_t = w_in.astype(F32).T.astype(BF)
    gain_a, rest = gain_row.astype(BF), gain_row - gain_row.astype(BF).astype(F32)
    gain_b = rest.astype(BF)
    gain_c = (rest - gain_b.astype(F32)).astype(BF)
    group_row = lax.broadcasted_iota(jnp.int32, (GROUP, 1), 0)
    gain_parts = [
        jnp.concatenate(
            [jnp.where(group_row == step, part_of.astype(F32), 0.0) for part_of in (gain_a, gain_b, gain_c)], axis=0
        ).astype(BF)
        for step in range(GROUP)
    ]
    col_ref[...] = jnp.zeros_like(col_ref)
    act_sum_ref[...] = jnp.zeros_like(act_sum_ref)

    def body(index, carry):
        start = pl.multiple_of(index * GROUP, GROUP)
        turned = pltpu.roll(left, (tile - start) % tile, 1)
        logits = jnp.zeros((3 * GROUP, tile), F32)
        for step in range(GROUP):
            pair_in = (turned[:, step : step + 1] + shifted).astype(BF)
            x = mm(w_in_t, pair_in)
            inner = CURVE + CUBIC * (x * x)
            bend = jnp.tanh(x * inner)
            lift = 1.0 + bend
            act = (x * lift).astype(BF)
            slope_ref[step] = lift + (1.0 - bend * bend) * (x * (3.0 * inner - 2.0 * CURVE))
            act_ref[step] = act
            logits = logits + mm(gain_parts[step], act)
        logits = logits[:GROUP] + logits[GROUP : 2 * GROUP] + logits[2 * GROUP :]
        logits = logits + logit_col_ref[pl.ds(start, GROUP), :] + logit_row
        logit_ref[pl.ds(start, GROUP), :] = logits
        mask = flag_col_ref[pl.ds(start, GROUP), :] * col_flags
        res = mask * (logits - target_wide[pl.ds(start, GROUP), :])
        res_ref[pl.ds(start, GROUP), :] = res
        high = res.astype(BF).astype(F32)
        low = res - high
        grow = jnp.zeros((2 * GROUP, hidden), F32)
        acts = jnp.zeros((2 * GROUP, hidden), F32)
        total = col_ref[...]
        for step in range(GROUP):
            slope = slope_ref[step]
            keep = group_row == step
            lhs = jnp.concatenate([jnp.where(keep, high, 0.0), jnp.where(keep, low, 0.0)], axis=0).astype(BF)
            grow = grow + mm(lhs, slope.astype(BF), NT)
            acts = acts + mm(lhs, act_ref[step], NT)
            total = total + slope * res[step : step + 1]
        col_ref[...] = total
        row_ref[pl.ds(start, GROUP), :] = grow[:GROUP] + grow[GROUP:]
        act_sum_ref[...] += acts
        return carry

    lax.fori_loop(0, tile // GROUP, body, 0)

    pred_ref[...] = logit_ref[...].astype(BF)
    res = res_ref[...]
    res_col = jnp.sum(res, axis=0, keepdims=True)
    res_row = to_row(jnp.sum(res, axis=1, keepdims=True))
    res_all = jnp.sum(res_row, axis=1, keepdims=True)
    row_part = row_ref[...] * gain_row
    col_part = col_ref[...] * gain
    act_sum = jnp.sum(act_sum_ref[...], axis=0, keepdims=True) * 0.5
    row_sums = head * res_row + mm_wide(w_in, row_part, NT)
    col_sums = head * res_col + mm_wide(w_in, col_part)
    left_low, right_low = left_ref[...], right.astype(BF)
    in_term = (
        mm_wide(left_low, row_part) + mm_wide(right_low, col_part, NT) + bias * jnp.sum(row_part, axis=0, keepdims=True)
    )
    w_out_t = w_out_ref[...].astype(F32).T
    head_term = jnp.sum(left * res_row + right * res_col + w_out_t * act_sum, axis=1, keepdims=True) + bias * res_all
    bias_sum = jnp.sum(row_sums, axis=1, keepdims=True)
    wide = jnp.zeros((channels, hidden), F32)
    lane = lax.broadcasted_iota(jnp.int32, (channels, hidden), 1)
    wide = jnp.where(lane == 1, head_term, wide)
    wide = jnp.where(lane == offset + 2, bias_sum, wide)
    flat = jnp.concatenate([wide] + [jnp.zeros_like(wide)] * (hidden // channels - 1), axis=0).T
    first = lax.broadcasted_iota(jnp.int32, (GROUP, hidden), 0) == 0
    small = jnp.concatenate([in_term, jnp.where(first, act_sum, flat[:GROUP])], axis=0)
    small_high = small.astype(BF).astype(F32)
    small_low = small - small_high
    owners = small.shape[0] // GROUP
    send_ref[...] = jnp.zeros_like(send_ref)
    for piece_index in range(3 * owners):
        source = small_low if piece_index // owners == 1 else small_high
        block = piece_index % owners
        send_ref[piece_index, part:, :] = source[block * GROUP : (block + 1) * GROUP].astype(BF)
    for quarter in range(bands // 2):
        send_ref[here * bands + quarter, :part, :] = row_sums[quarter * part : (quarter + 1) * part].astype(BF)

    @pl.when(there < rows)
    def _():
        for quarter in range(bands // 2):
            send_ref[there * bands + bands // 2 + quarter, :part, :] = col_sums[
                quarter * part : (quarter + 1) * part
            ].astype(BF)


def total_kernel(info_ref, recv_ref, send_ref):
    devices, height, width = recv_ref.shape
    total = recv_ref[0].astype(F32)
    for source in range(1, devices):
        total = total + recv_ref[source].astype(F32)
    low = total - total.astype(BF).astype(F32)
    row = lax.broadcasted_iota(jnp.int32, (height, width), 0)
    use_low = jnp.logical_and(info_ref[0] == 2, row >= height - GROUP)
    piece = jnp.where(use_low, low, total).astype(BF)
    for target in range(devices):
        send_ref[target] = piece


def finish_kernel(
    info_ref, recv_ref, emb_ref, wl_ref, wr_ref, w_head_ref, share_ref, grad_emb_ref, in_ref, out_ref, head_ref, bias_ref
):
    rows = emb_ref.shape[0]
    devices, height, width = recv_ref.shape
    bands = devices // rows
    part = height - GROUP
    channels = in_ref.shape[0]
    hidden = out_ref.shape[0]

    def grads(row):
        return jnp.concatenate([recv_ref[row * bands + band, :part, :].astype(F32) for band in range(bands)], axis=0)

    def body(row, total):
        return total + mm(grads(row).astype(BF), emb_ref[row])

    share_ref[...] = lax.fori_loop(0, rows, body, jnp.zeros(share_ref.shape, F32), unroll=rows <= 8)
    own = grads(info_ref[0]).astype(BF)
    share = pl.ds(pl.multiple_of(info_ref[1] * width, width), width)
    weights = jnp.concatenate([wl_ref[share, :].astype(F32), wr_ref[share, :].astype(F32)], axis=1).astype(BF)
    grad_emb_ref[...] = mm(weights, own).T.astype(BF)
    owners = channels // GROUP + 1
    small = [
        recv_ref[block, part:, :].astype(F32)
        + recv_ref[owners + block, part:, :].astype(F32)
        + recv_ref[2 * owners + block, part:, :].astype(F32)
        for block in range(owners)
    ]
    in_ref[...] = jnp.concatenate(small[:-1], axis=0)
    last = small[-1]
    turned = jnp.concatenate([last, jnp.zeros((hidden - GROUP, hidden), F32)], axis=0).T
    out_ref[...] = turned[:, :1] * w_head_ref[...]
    head_ref[...] = last[1:2, :channels]
    bias_ref[...] = turned[:channels, 2 : 2 + bias_ref.shape[1]]


def arrange_kernel(info_ref, own_ref, other_ref, left_ref, right_ref):
    channels = left_ref.shape[1]
    width = own_ref.shape[1]
    for ref, index in ((own_ref, info_ref[0]), (other_ref, 1 - info_ref[0])):
        turned = ref[...].T
        place = pl.ds(pl.multiple_of(index * width, width), width)
        left_ref[place, :] = turned[:, :channels]
        right_ref[place, :] = turned[:, channels:]


def vmem():
    return pl.BlockSpec(memory_space=pltpu.VMEM)


def smem():
    return pl.BlockSpec(memory_space=pltpu.SMEM)


def call(kernel, outs, ins, scratch=(), name=None):
    return pl.pallas_call(
        kernel,
        out_shape=[jax.ShapeDtypeStruct(shape, kind) for shape, kind in outs],
        in_specs=ins,
        out_specs=[vmem()] * len(outs),
        scratch_shapes=[pltpu.VMEM(shape, kind) for shape, kind in scratch],
        name=name,
    )


def exchange(value, axes):
    return lax.all_to_all(value, axes, 0, 0, tiled=True)


def on_device(embedding, w_left, w_right, w_in, w_out, w_head, dist_bias, offsets, valid_bins, target):
    rows, bands = lax.axis_size("rows"), lax.axis_size("band")
    devices = rows * bands
    bins, features = embedding.shape
    channels, hidden = w_in.shape
    tile = target.shape[-1]
    part = 2 * channels // bands
    owners = channels // GROUP + 1
    half = features // HALVES
    row_index, band_index = lax.axis_index("rows"), lax.axis_index("band")
    device_index = row_index * bands + band_index
    half_index = band_index % HALVES
    flags = valid_bins.reshape(1, bins)
    head_row = w_head.reshape(1, channels)

    left, send = call(
        project_kernel,
        [((channels, bins), BF), ((rows, channels + GROUP, bins), BF)],
        [vmem()] * 4,
        name="project",
    )(embedding, w_left, w_right, flags)
    received = exchange(send, "rows")
    embedding, received = lax.optimization_barrier((embedding, received))
    emb_half = lax.dynamic_slice_in_dim(embedding, half_index * half, half, 1)
    emb_all = exchange(jnp.broadcast_to(emb_half[None], (rows, bins, half)), "rows")

    info = jnp.stack([row_index, offsets[0, 0]]).astype(jnp.int32)
    predicted, send = call(
        tile_kernel,
        [((tile, tile), BF), ((devices, part + GROUP, tile), BF)],
        [smem()] + [vmem()] * 8,
        [
            ((tile, tile), F32),
            ((GROUP, hidden, tile), BF),
            ((GROUP, hidden, tile), F32),
            ((tile, tile), F32),
            ((tile, tile), F32),
            ((tile, hidden), F32),
            ((hidden, tile), F32),
            ((2 * GROUP, hidden), F32),
            ((tile, 1), F32),
            ((tile, 1), F32),
        ],
        name="tile",
    )(info, left, received, flags, target.reshape(tile, tile), w_in, w_out, head_row, dist_bias)
    partial = exchange(send, ("rows", "band"))
    group = (device_index // owners).astype(jnp.int32).reshape(1)
    (send,) = call(
        total_kernel, [(partial.shape, BF)], [smem(), vmem()], name="total"
    )(group, partial)
    complete = exchange(send, ("rows", "band"))
    place = jnp.stack([row_index, band_index]).astype(jnp.int32)
    share, grad_embedding, grad_in, grad_out, grad_head, grad_bias = call(
        finish_kernel,
        [
            ((2 * channels, half), F32),
            ((bins, features // bands), BF),
            ((channels, hidden), F32),
            ((hidden, channels), F32),
            ((1, channels), F32),
            (dist_bias.shape, F32),
        ],
        [smem()] + [vmem()] * 5,
        name="finish",
    )(place, complete, emb_all, w_left, w_right, head_row)
    other = lax.ppermute(share, "band", [(source, source ^ 1) for source in range(bands)])
    grad_left, grad_right = call(
        arrange_kernel,
        [(w_left.shape, F32), (w_right.shape, F32)],
        [smem(), vmem(), vmem()],
        name="arrange",
    )(half_index.astype(jnp.int32).reshape(1), share, other)
    return (
        predicted.reshape(target.shape),
        grad_embedding,
        grad_left,
        grad_right,
        grad_in,
        grad_out,
        grad_head.reshape(channels),
        grad_bias,
    )


def solution(mesh):
    placed = (
        P("rows", None),
        P(),
        P(),
        P(),
        P(),
        P(),
        P(),
        P("rows", "band"),
        P("rows"),
        P("rows", "band", None, None),
    )
    return jax.shard_map(
        on_device,
        mesh=mesh,
        in_specs=placed,
        out_specs=(P("rows", "band", None, None), P("rows", "band"), P(), P(), P(), P(), P(), P()),
        check_vma=False,
    )
```

```python
import functools
import math

import jax
import jax.numpy as jnp
from jax import lax
from jax.experimental import pallas as pl
from jax.experimental.pallas import tpu as pltpu
from jax.sharding import PartitionSpec as P


BF = jnp.bfloat16
F32 = jnp.float32
CURVE = math.sqrt(2.0 / math.pi)
CUBIC = 0.044715 * CURVE
GROUP = 8
HALVES = 2
SMALL = 1 << 20
NT = (((1,), (1,)), ((), ()))
NN = (((1,), (0,)), ((), ()))


def mm(a, b, dims=NN):
    return lax.dot_general(a, b, dims, preferred_element_type=F32)


def split(x):
    high = x.astype(BF)
    return high, (x - high.astype(F32)).astype(BF)


def mm_wide(a, b, dims=NN):
    high, low = split(b)
    return mm(a, high, dims) + mm(a, low, dims)


def eye(count):
    return lax.broadcasted_iota(jnp.int32, (count, count), 0) == lax.broadcasted_iota(
        jnp.int32, (count, count), 1
    )


def to_col(row):
    count = row.shape[1]
    return jnp.sum(jnp.where(eye(count), jnp.broadcast_to(row, (count, count)), 0.0), axis=1, keepdims=True)


def to_row(col):
    count = col.shape[0]
    return jnp.sum(jnp.where(eye(count), jnp.broadcast_to(col, (count, count)), 0.0), axis=0, keepdims=True)


def project_kernel(emb_ref, wl_ref, wr_ref, flags_ref, left_ref, send_ref, share_ref):
    emb = emb_ref[...]
    bins = emb.shape[0]
    left_ref[...] = mm(wl_ref[...], emb, NT).astype(BF)
    flags = jnp.broadcast_to(flags_ref[...].astype(F32), (GROUP, bins))
    piece = jnp.concatenate([mm(wr_ref[...], emb, NT), flags], axis=0).astype(BF)
    width = share_ref.shape[2]
    start = pl.multiple_of(lax.rem(lax.axis_index("band"), HALVES) * width, width)
    share = emb_ref[:, pl.ds(start, width)]

    def body(row, carry):
        send_ref[row] = piece
        share_ref[row] = share
        return carry

    lax.fori_loop(0, send_ref.shape[0], body, 0, unroll=send_ref.shape[0] <= 8)


def tile_kernel(
    offset_ref,
    left_ref,
    recv_ref,
    flags_ref,
    target_ref,
    w_in_ref,
    w_out_ref,
    w_head_ref,
    bias_ref,
    pred_ref,
    send_ref,
    target_wide,
    act_ref,
    slope_ref,
    logit_ref,
    res_ref,
    row_ref,
    col_ref,
    act_sum_ref,
    logit_col_ref,
    flag_col_ref,
):
    channels, hidden = w_in_ref.shape
    tile = target_ref.shape[0]
    noff = bias_ref.shape[0]
    rows = recv_ref.shape[0]
    bands = send_ref.shape[0] // rows
    part = 2 * channels // bands
    here, offset = lax.axis_index("rows"), offset_ref[0, 0]
    there = here + offset
    inside = (there < rows).astype(F32)
    piece = recv_ref[jnp.minimum(there, rows - 1)].astype(F32) * inside
    right = piece[:channels]
    col_flags = piece[channels : channels + 1] * (1.0 / (noff * tile))
    left = left_ref[...].astype(F32)
    off_row = lax.broadcasted_iota(jnp.int32, (noff, channels), 0)
    bias = to_col(jnp.sum(jnp.where(off_row == offset, bias_ref[...], 0.0), axis=0, keepdims=True))
    head_row = w_head_ref[...]
    head = to_col(head_row)
    w_out_t = w_out_ref[...].astype(F32)
    gain_row = jnp.sum(w_out_t * head, axis=0, keepdims=True) * 0.5
    gain = to_col(gain_row)
    logit_col_ref[...] = to_col(jnp.sum((left + bias) * head, axis=0, keepdims=True))
    logit_row = jnp.sum(right * head, axis=0, keepdims=True)
    flag_col_ref[...] = to_col(flags_ref[...].astype(F32))
    target_wide[...] = target_ref[...].astype(F32)
    shifted = right + bias
    w_in = w_in_ref[...]
    w_in_t = w_in.astype(F32).T.astype(BF)
    gain_a, rest = gain_row.astype(BF), gain_row - gain_row.astype(BF).astype(F32)
    gain_b = rest.astype(BF)
    gain_c = (rest - gain_b.astype(F32)).astype(BF)
    group_row = lax.broadcasted_iota(jnp.int32, (GROUP, 1), 0)
    gain_parts = [
        jnp.concatenate(
            [jnp.where(group_row == step, part_of.astype(F32), 0.0) for part_of in (gain_a, gain_b, gain_c)], axis=0
        ).astype(BF)
        for step in range(GROUP)
    ]
    col_ref[...] = jnp.zeros_like(col_ref)
    act_sum_ref[...] = jnp.zeros_like(act_sum_ref)

    def body(index, carry):
        start = pl.multiple_of(index * GROUP, GROUP)
        turned = pltpu.roll(left, (tile - start) % tile, 1)
        logits = jnp.zeros((3 * GROUP, tile), F32)
        for step in range(GROUP):
            pair_in = (turned[:, step : step + 1] + shifted).astype(BF)
            x = mm(w_in_t, pair_in)
            inner = CURVE + CUBIC * (x * x)
            bend = jnp.tanh(x * inner)
            lift = 1.0 + bend
            act = (x * lift).astype(BF)
            slope_ref[step] = lift + (1.0 - bend * bend) * (x * (3.0 * inner - 2.0 * CURVE))
            act_ref[step] = act
            logits = logits + mm(gain_parts[step], act)
        logits = logits[:GROUP] + logits[GROUP : 2 * GROUP] + logits[2 * GROUP :]
        logits = logits + logit_col_ref[pl.ds(start, GROUP), :] + logit_row
        logit_ref[pl.ds(start, GROUP), :] = logits
        mask = flag_col_ref[pl.ds(start, GROUP), :] * col_flags
        res = mask * (logits - target_wide[pl.ds(start, GROUP), :])
        res_ref[pl.ds(start, GROUP), :] = res
        high = res.astype(BF).astype(F32)
        low = res - high
        grow = jnp.zeros((2 * GROUP, hidden), F32)
        acts = jnp.zeros((2 * GROUP, hidden), F32)
        total = col_ref[...]
        for step in range(GROUP):
            slope = slope_ref[step]
            keep = group_row == step
            lhs = jnp.concatenate([jnp.where(keep, high, 0.0), jnp.where(keep, low, 0.0)], axis=0).astype(BF)
            grow = grow + mm(lhs, slope.astype(BF), NT)
            acts = acts + mm(lhs, act_ref[step], NT)
            total = total + slope * res[step : step + 1]
        col_ref[...] = total
        row_ref[pl.ds(start, GROUP), :] = grow[:GROUP] + grow[GROUP:]
        act_sum_ref[...] += acts
        return carry

    lax.fori_loop(0, tile // GROUP, body, 0)

    pred_ref[...] = logit_ref[...].astype(BF)
    res = res_ref[...]
    res_col = jnp.sum(res, axis=0, keepdims=True)
    res_row = to_row(jnp.sum(res, axis=1, keepdims=True))
    res_all = jnp.sum(res_row, axis=1, keepdims=True)
    row_part = row_ref[...] * gain_row
    col_part = col_ref[...] * gain
    act_sum = jnp.sum(act_sum_ref[...], axis=0, keepdims=True) * 0.5
    row_sums = head * res_row + mm_wide(w_in, row_part, NT)
    col_sums = head * res_col + mm_wide(w_in, col_part)
    left_low, right_low = left_ref[...], right.astype(BF)
    in_term = (
        mm_wide(left_low, row_part) + mm_wide(right_low, col_part, NT) + bias * jnp.sum(row_part, axis=0, keepdims=True)
    )
    head_term = jnp.sum(left * res_row + right * res_col + w_out_t * act_sum, axis=1, keepdims=True) + bias * res_all
    bias_sum = jnp.sum(row_sums, axis=1, keepdims=True)
    wide = jnp.zeros((channels, hidden), F32)
    lane = lax.broadcasted_iota(jnp.int32, (channels, hidden), 1)
    wide = jnp.where(lane == 1, head_term, wide)
    wide = jnp.where(lane == offset + 2, bias_sum, wide)
    flat = jnp.concatenate([wide] + [jnp.zeros_like(wide)] * (hidden // channels - 1), axis=0).T
    first = lax.broadcasted_iota(jnp.int32, (GROUP, hidden), 0) == 0
    small = jnp.concatenate([in_term, jnp.where(first, act_sum, flat[:GROUP])], axis=0)
    small_high = small.astype(BF).astype(F32)
    small_low = small - small_high
    owners = small.shape[0] // GROUP
    send_ref[...] = jnp.zeros_like(send_ref)
    for piece_index in range(3 * owners):
        source = small_low if piece_index // owners == 1 else small_high
        block = piece_index % owners
        send_ref[piece_index, part:, :] = source[block * GROUP : (block + 1) * GROUP].astype(BF)
    for quarter in range(bands // 2):
        send_ref[here * bands + quarter, :part, :] = row_sums[quarter * part : (quarter + 1) * part].astype(BF)

    @pl.when(there < rows)
    def _():
        for quarter in range(bands // 2):
            send_ref[there * bands + bands // 2 + quarter, :part, :] = col_sums[
                quarter * part : (quarter + 1) * part
            ].astype(BF)


def total_kernel(owners, recv_ref, send_ref):
    _, height, width = recv_ref.shape
    total = jnp.sum(recv_ref[...].astype(F32), axis=0)
    index = lax.axis_index("rows") * lax.axis_size("band") + lax.axis_index("band")
    low = total - total.astype(BF).astype(F32)
    row = lax.broadcasted_iota(jnp.int32, (height, width), 0)
    third = jnp.logical_and(index >= 2 * owners, index < 3 * owners)
    use_low = jnp.logical_and(third, row >= height - GROUP)
    send_ref[...] = jnp.broadcast_to(jnp.where(use_low, low, total).astype(BF)[None], send_ref.shape)


def finish_kernel(
    recv_ref, emb_ref, wl_ref, wr_ref, w_head_ref, share_ref, grad_emb_ref, in_ref, out_ref, head_ref, bias_ref
):
    rows = emb_ref.shape[0]
    devices, height, width = recv_ref.shape
    bands = devices // rows
    part = height - GROUP
    channels = in_ref.shape[0]

    def grads(row):
        return jnp.concatenate([recv_ref[row * bands + band, :part, :].astype(F32) for band in range(bands)], axis=0)

    def body(row, total):
        return total + mm(grads(row).astype(BF), emb_ref[row])

    share_ref[...] = lax.fori_loop(0, rows, body, jnp.zeros(share_ref.shape, F32), unroll=rows <= 8)
    own = grads(lax.axis_index("rows")).T.astype(BF)
    share = pl.ds(pl.multiple_of(lax.axis_index("band") * width, width), width)
    weights = jnp.concatenate([wl_ref[:, share], wr_ref[:, share]], axis=0)
    grad_emb_ref[...] = mm(own, weights).astype(BF)
    owners = channels // GROUP + 1
    small = [
        recv_ref[block, part:, :].astype(F32)
        + recv_ref[owners + block, part:, :].astype(F32)
        + recv_ref[2 * owners + block, part:, :].astype(F32)
        for block in range(owners)
    ]
    in_ref[...] = jnp.concatenate(small[:-1], axis=0)
    last = small[-1]
    out_ref[...] = last[:1] * to_col(w_head_ref[...])
    head_ref[...] = last[1:2, :channels]
    bias_ref[...] = last[2 : 2 + bias_ref.shape[0], :channels]


def arrange_kernel(own_ref, other_ref, left_ref, right_ref):
    channels = left_ref.shape[0]
    width = own_ref.shape[1]
    half = lax.rem(lax.axis_index("band"), HALVES)
    for ref, index in ((own_ref, half), (other_ref, 1 - half)):
        place = pl.ds(pl.multiple_of(index * width, width), width)
        left_ref[:, place] = ref[:channels]
        right_ref[:, place] = ref[channels:]


def vmem():
    return pl.BlockSpec(memory_space=pltpu.VMEM)


def smem():
    return pl.BlockSpec(memory_space=pltpu.SMEM)


def fits(shape, kind):
    return math.prod(shape) * jnp.dtype(kind).itemsize <= SMALL


def near(value):
    return pltpu.with_memory_space_constraint(value, pltpu.VMEM) if fits(value.shape, value.dtype) else value


def call(kernel, outs, args, first=None, scratch=()):
    return pl.pallas_call(
        kernel,
        out_shape=[
            pltpu.VMEM(shape, kind) if inner and fits(shape, kind) else jax.ShapeDtypeStruct(shape, kind) for shape, kind, inner in outs
        ],
        in_specs=[first or vmem()] + [vmem()] * (len(args) - 1),
        out_specs=[vmem()] * len(outs),
        scratch_shapes=[pltpu.VMEM(shape, kind) for shape, kind in scratch],
    )(*args)


def exchange(value, axes):
    return lax.all_to_all(value, axes, 0, 0, tiled=True)


def on_device(embedding, w_left, w_right, w_in, w_out, w_head, dist_bias, offsets, valid_bins, target):
    rows, bands = lax.axis_size("rows"), lax.axis_size("band")
    devices = rows * bands
    bins, features = embedding.shape
    channels, hidden = w_in.shape
    tile = target.shape[-1]
    part = 2 * channels // bands
    owners = channels // GROUP + 1
    half = features // HALVES
    flags = valid_bins.reshape(1, bins)
    head_row = w_head.reshape(1, channels)

    left, send, share = call(
        project_kernel,
        [((channels, bins), BF, True), ((rows, channels + GROUP, bins), BF, True), ((rows, bins, half), BF, True)],
        (embedding, w_left.T, w_right.T, flags),
    )
    received = exchange(send, "rows")
    share, received = lax.optimization_barrier((share, received))
    emb_all = exchange(share, "rows")
    predicted, send = call(
        tile_kernel,
        [((tile, tile), BF, False), ((devices, part + GROUP, tile), BF, True)],
        (offsets, near(left), near(received), flags, target.reshape(tile, tile), w_in, w_out.T, head_row, dist_bias.T),
        smem(),
        [
            ((tile, tile), F32),
            ((GROUP, hidden, tile), BF),
            ((GROUP, hidden, tile), F32),
            ((tile, tile), F32),
            ((tile, tile), F32),
            ((tile, hidden), F32),
            ((hidden, tile), F32),
            ((2 * GROUP, hidden), F32),
            ((tile, 1), F32),
            ((tile, 1), F32),
        ],
    )
    send, emb_all = lax.optimization_barrier((send, emb_all))
    partial = exchange(send, ("rows", "band"))
    (send,) = call(functools.partial(total_kernel, owners), [(partial.shape, BF, True)], (near(partial),))
    complete = exchange(send, ("rows", "band"))
    mine, grad_embedding, grad_in, grad_out, grad_head, grad_bias = call(
        finish_kernel,
        [
            ((2 * channels, half), F32, True),
            ((bins, features // bands), BF, False),
            ((channels, hidden), F32, False),
            ((channels, hidden), F32, False),
            ((1, channels), F32, False),
            (dist_bias.shape[::-1], F32, False),
        ],
        (near(complete), near(emb_all), w_left.T, w_right.T, head_row),
    )
    other = lax.ppermute(mine, "band", [(source, source ^ 1) for source in range(bands)])
    grad_left, grad_right = call(arrange_kernel, [((channels, features), F32, False)] * 2, (near(mine), near(other)))
    return (
        predicted.reshape(target.shape),
        grad_embedding,
        grad_left.T,
        grad_right.T,
        grad_in,
        grad_out.T,
        grad_head.reshape(channels),
        grad_bias.T,
    )


def solution(mesh):
    placed = (
        P("rows", None),
        P(),
        P(),
        P(),
        P(),
        P(),
        P(),
        P("rows", "band"),
        P("rows"),
        P("rows", "band", None, None),
    )

    return jax.shard_map(
        on_device,
        mesh=mesh,
        in_specs=placed,
        out_specs=(P("rows", "band", None, None), P("rows", "band"), P(), P(), P(), P(), P(), P()),
        check_vma=False,
    )
```

```python
import functools
import math

import jax
import jax.numpy as jnp
from jax import lax
from jax.experimental import pallas as pl
from jax.experimental.pallas import tpu as pltpu
from jax.sharding import PartitionSpec as P


BF = jnp.bfloat16
F32 = jnp.float32
CURVE = math.sqrt(2.0 / math.pi)
STRETCH = (0.044715 * CURVE) ** (1.0 / 3.0)
LINEAR = CURVE / STRETCH
GROUP = 8
HALVES = 2
SMALL = 1 << 20
NT = (((1,), (1,)), ((), ()))
NN = (((1,), (0,)), ((), ()))


def mm(a, b, dims=NN):
    return lax.dot_general(a, b, dims, preferred_element_type=F32)


def split(x):
    high = x.astype(BF)
    return high, (x - high.astype(F32)).astype(BF)


def mm_wide(a, b, dims=NN):
    high, low = split(b)
    return mm(a, high, dims) + mm(a, low, dims)


def eye(count):
    return lax.broadcasted_iota(jnp.int32, (count, count), 0) == lax.broadcasted_iota(
        jnp.int32, (count, count), 1
    )


def to_col(row):
    count = row.shape[1]
    return jnp.sum(jnp.where(eye(count), jnp.broadcast_to(row, (count, count)), 0.0), axis=1, keepdims=True)


def to_row(col):
    count = col.shape[0]
    return jnp.sum(jnp.where(eye(count), jnp.broadcast_to(col, (count, count)), 0.0), axis=0, keepdims=True)


def project_kernel(emb_ref, wl_ref, wr_ref, flags_ref, left_ref, send_ref, share_ref):
    emb = emb_ref[...]
    bins = emb.shape[0]
    left_ref[...] = mm(wl_ref[...], emb, NT).astype(BF)
    flags = jnp.broadcast_to(flags_ref[...].astype(F32), (GROUP, bins))
    piece = jnp.concatenate([mm(wr_ref[...], emb, NT), flags], axis=0).astype(BF)
    width = share_ref.shape[2]
    start = pl.multiple_of(lax.rem(lax.axis_index("band"), HALVES) * width, width)
    share = emb_ref[:, pl.ds(start, width)]

    def body(row, carry):
        send_ref[row] = piece
        share_ref[row] = share
        return carry

    lax.fori_loop(0, send_ref.shape[0], body, 0, unroll=send_ref.shape[0] <= 8)


def tile_kernel(
    offset_ref,
    left_ref,
    recv_ref,
    flags_ref,
    target_ref,
    w_in_ref,
    w_out_ref,
    w_head_ref,
    bias_ref,
    pred_ref,
    send_ref,
    target_wide,
    act_ref,
    slope_ref,
    logit_ref,
    res_ref,
    col_ref,
    product_ref,
    pick_ref,
    sums_ref,
    logit_col_ref,
    flag_col_ref,
):
    channels, hidden = w_in_ref.shape
    tile = target_ref.shape[0]
    noff = bias_ref.shape[0]
    rows = recv_ref.shape[0]
    bands = send_ref.shape[0] // rows
    part = 2 * channels // bands
    here, offset = lax.axis_index("rows"), offset_ref[0, 0]
    there = here + offset
    inside = (there < rows).astype(F32)
    piece = recv_ref[jnp.minimum(there, rows - 1)].astype(F32) * inside
    right = piece[:channels]
    col_flags = piece[channels : channels + 1] * (1.0 / (noff * tile))
    left = left_ref[...].astype(F32)
    off_row = lax.broadcasted_iota(jnp.int32, (noff, channels), 0)
    bias = to_col(jnp.sum(jnp.where(off_row == offset, bias_ref[...], 0.0), axis=0, keepdims=True))
    head_row = w_head_ref[...]
    head = to_col(head_row)
    w_out_t = w_out_ref[...].astype(F32)
    gain_row = jnp.sum(w_out_t * head, axis=0, keepdims=True)
    gain = to_col(gain_row) * 0.5
    gain_row = gain_row * (0.5 / STRETCH)
    logit_col_ref[...] = to_col(jnp.sum((left + bias) * head, axis=0, keepdims=True))
    logit_row = jnp.sum(right * head, axis=0, keepdims=True)
    flag_col_ref[...] = to_col(flags_ref[...].astype(F32))
    target_wide[...] = target_ref[...].astype(F32)
    shifted = right + bias
    w_in = w_in_ref[...]
    w_high, w_low = split(w_in.astype(F32).T * STRETCH)
    w_both = jnp.concatenate([w_high, w_low], axis=1)
    gain_high = gain_row.astype(BF).astype(F32)
    gain_low = gain_row - gain_high
    group_row = lax.broadcasted_iota(jnp.int32, (GROUP, 1), 0)
    gain_parts = [
        jnp.concatenate([jnp.where(group_row == step, piece, 0.0) for piece in (gain_high, gain_low)], axis=0).astype(BF)
        for step in range(GROUP)
    ]
    col_ref[...] = jnp.zeros_like(col_ref)
    chosen = lax.broadcasted_iota(jnp.int32, pick_ref.shape, 0) // tile
    lane_of = lax.broadcasted_iota(jnp.int32, pick_ref.shape, 1)
    pick_ref[...] = jnp.where(jnp.minimum(chosen, GROUP) == lane_of, 1.0, 0.0).astype(BF)
    groups = tile // GROUP

    def start_of(group):
        return pl.multiple_of(group * GROUP, GROUP)

    def turn(group):
        return pltpu.roll(left, lax.rem(tile - start_of(group), tile), 1)

    def forward(turned, step, slot, logits):
        pair_in = (turned[:, step : step + 1] + shifted).astype(BF)
        x = mm(w_both, jnp.concatenate([pair_in, pair_in], axis=0))
        square = x * x
        inner = square + LINEAR
        bend = jnp.tanh(x * inner)
        lift = 1.0 + bend
        act = x * lift
        slope_ref[slot, step] = lift + (act * (1.0 - bend)) * (inner + (square + square))
        act = act.astype(BF)
        act_ref[slot, step] = act
        return logits + mm(gain_parts[step], act)

    def settle(group, logits):
        at = pl.ds(start_of(group), GROUP)
        logits = logits[:GROUP] + logits[GROUP:]
        logits = logits + logit_col_ref[at, :] + logit_row
        logit_ref[at, :] = logits
        res_ref[at, :] = flag_col_ref[at, :] * col_flags * (logits - target_wide[at, :])

    def backward(res, res_low, step, slot, total):
        product = slope_ref[slot, step] * res[step : step + 1]
        product_ref[slot, :, step * tile : (step + 1) * tile] = product.astype(BF)
        product_ref[slot, :, (GROUP + step) * tile : (GROUP + step + 1) * tile] = (
            act_ref[slot, step] * res_low[step : step + 1]
        )
        return total + product

    def none():
        return jnp.zeros((2 * GROUP, tile), F32)

    logits = none()
    turned = turn(0)
    for step in range(GROUP):
        logits = forward(turned, step, 0, logits)
    settle(0, logits)

    def body(index, carry):
        for slot in range(2):
            group = 2 * index + slot
            following = lax.rem(group + 1, groups)
            at = pl.ds(start_of(group), GROUP)
            res = res_ref[at, :]
            res_low = res.astype(BF)
            total = col_ref[...]
            turned = turn(following)
            logits = none()
            for step in range(GROUP):
                logits = forward(turned, step, 1 - slot, logits)
                total = backward(res, res_low, step, slot, total)
            col_ref[...] = total
            sums_ref[group] = mm(product_ref[slot], pick_ref[...])
            settle(following, logits)
        return carry

    lax.fori_loop(0, groups // 2, body, 0)

    pred_ref[...] = logit_ref[...].astype(BF)
    res = res_ref[...]
    res_col = jnp.sum(res, axis=0, keepdims=True)
    res_row = to_row(jnp.sum(res, axis=1, keepdims=True))
    res_all = jnp.sum(res_row, axis=1, keepdims=True)
    row_sum = jnp.zeros((hidden, tile), F32)
    act_sum = jnp.zeros((hidden, tile), F32)
    lane = lax.broadcasted_iota(jnp.int32, (hidden, tile), 1)
    for group in range(groups):
        sums = sums_ref[group]
        act_sum = act_sum + sums
        moved = pltpu.roll(sums, group * GROUP, 1) if group else sums
        row_sum = jnp.where(lane // GROUP == group, moved, row_sum)
    row_part = row_sum * gain
    act_sum = jnp.sum(jnp.where(lane == GROUP, act_sum, 0.0), axis=1, keepdims=True) * (0.5 / STRETCH)
    act_sum = to_row(act_sum)
    col_part = col_ref[...] * gain
    row_sums = head * res_row + mm_wide(w_in, row_part)
    col_sums = head * res_col + mm_wide(w_in, col_part)
    left_low, right_low = left_ref[...], right.astype(BF)
    in_term = (
        mm_wide(left_low, row_part, NT) + mm_wide(right_low, col_part, NT) + bias * to_row(jnp.sum(row_part, axis=1, keepdims=True))
    )
    head_term = jnp.sum(left * res_row + right * res_col + w_out_t * act_sum, axis=1, keepdims=True) + bias * res_all
    bias_sum = jnp.sum(row_sums, axis=1, keepdims=True)
    wide = jnp.zeros((channels, hidden), F32)
    lane = lax.broadcasted_iota(jnp.int32, (channels, hidden), 1)
    wide = jnp.where(lane == 1, head_term, wide)
    wide = jnp.where(lane == offset + 2, bias_sum, wide)
    flat = jnp.concatenate([wide] + [jnp.zeros_like(wide)] * (hidden // channels - 1), axis=0).T
    first = lax.broadcasted_iota(jnp.int32, (GROUP, hidden), 0) == 0
    small = jnp.concatenate([in_term, jnp.where(first, act_sum, flat[:GROUP])], axis=0)
    small_high = small.astype(BF).astype(F32)
    small_low = small - small_high
    owners = small.shape[0] // GROUP
    send_ref[...] = jnp.zeros_like(send_ref)
    for piece_index in range(3 * owners):
        source = small_low if piece_index // owners == 1 else small_high
        block = piece_index % owners
        send_ref[piece_index, part:, :] = source[block * GROUP : (block + 1) * GROUP].astype(BF)
    for quarter in range(bands // 2):
        send_ref[here * bands + quarter, :part, :] = row_sums[quarter * part : (quarter + 1) * part].astype(BF)

    @pl.when(there < rows)
    def _():
        for quarter in range(bands // 2):
            send_ref[there * bands + bands // 2 + quarter, :part, :] = col_sums[
                quarter * part : (quarter + 1) * part
            ].astype(BF)


def total_kernel(owners, recv_ref, send_ref):
    _, height, width = recv_ref.shape
    total = jnp.sum(recv_ref[...].astype(F32), axis=0)
    index = lax.axis_index("rows") * lax.axis_size("band") + lax.axis_index("band")
    low = total - total.astype(BF).astype(F32)
    row = lax.broadcasted_iota(jnp.int32, (height, width), 0)
    third = jnp.logical_and(index >= 2 * owners, index < 3 * owners)
    use_low = jnp.logical_and(third, row >= height - GROUP)
    send_ref[...] = jnp.broadcast_to(jnp.where(use_low, low, total).astype(BF)[None], send_ref.shape)


def finish_kernel(
    recv_ref, emb_ref, wl_ref, wr_ref, w_head_ref, share_ref, grad_emb_ref, in_ref, out_ref, head_ref, bias_ref
):
    rows = emb_ref.shape[0]
    devices, height, width = recv_ref.shape
    bands = devices // rows
    part = height - GROUP
    channels = in_ref.shape[0]

    def grads(row):
        return jnp.concatenate([recv_ref[row * bands + band, :part, :].astype(F32) for band in range(bands)], axis=0)

    def body(row, total):
        return total + mm(grads(row).astype(BF), emb_ref[row])

    share_ref[...] = lax.fori_loop(0, rows, body, jnp.zeros(share_ref.shape, F32), unroll=rows <= 8)
    own = grads(lax.axis_index("rows")).T.astype(BF)
    share = pl.ds(pl.multiple_of(lax.axis_index("band") * width, width), width)
    weights = jnp.concatenate([wl_ref[:, share], wr_ref[:, share]], axis=0)
    grad_emb_ref[...] = mm(own, weights).astype(BF)
    owners = channels // GROUP + 1
    small = [
        recv_ref[block, part:, :].astype(F32)
        + recv_ref[owners + block, part:, :].astype(F32)
        + recv_ref[2 * owners + block, part:, :].astype(F32)
        for block in range(owners)
    ]
    in_ref[...] = jnp.concatenate(small[:-1], axis=0)
    last = small[-1]
    out_ref[...] = last[:1] * to_col(w_head_ref[...])
    head_ref[...] = last[1:2, :channels]
    bias_ref[...] = last[2 : 2 + bias_ref.shape[0], :channels]


def arrange_kernel(own_ref, other_ref, left_ref, right_ref):
    channels = left_ref.shape[0]
    width = own_ref.shape[1]
    half = lax.rem(lax.axis_index("band"), HALVES)
    for ref, index in ((own_ref, half), (other_ref, 1 - half)):
        place = pl.ds(pl.multiple_of(index * width, width), width)
        left_ref[:, place] = ref[:channels]
        right_ref[:, place] = ref[channels:]


def vmem():
    return pl.BlockSpec(memory_space=pltpu.VMEM)


def smem():
    return pl.BlockSpec(memory_space=pltpu.SMEM)


def fits(shape, kind):
    return math.prod(shape) * jnp.dtype(kind).itemsize <= SMALL


def near(value):
    return pltpu.with_memory_space_constraint(value, pltpu.VMEM) if fits(value.shape, value.dtype) else value


def call(kernel, outs, args, first=None, scratch=()):
    return pl.pallas_call(
        kernel,
        out_shape=[
            pltpu.VMEM(shape, kind) if inner and fits(shape, kind) else jax.ShapeDtypeStruct(shape, kind) for shape, kind, inner in outs
        ],
        in_specs=[first or vmem()] + [vmem()] * (len(args) - 1),
        out_specs=[vmem()] * len(outs),
        scratch_shapes=[pltpu.VMEM(shape, kind) for shape, kind in scratch],
    )(*args)


def exchange(value, axes):
    return lax.all_to_all(value, axes, 0, 0, tiled=True)


def on_device(embedding, w_left, w_right, w_in, w_out, w_head, dist_bias, offsets, valid_bins, target):
    rows, bands = lax.axis_size("rows"), lax.axis_size("band")
    devices = rows * bands
    bins, features = embedding.shape
    channels, hidden = w_in.shape
    tile = target.shape[-1]
    part = 2 * channels // bands
    owners = channels // GROUP + 1
    half = features // HALVES
    flags = valid_bins.reshape(1, bins)
    head_row = w_head.reshape(1, channels)

    left, send, share = call(
        project_kernel,
        [((channels, bins), BF, True), ((rows, channels + GROUP, bins), BF, True), ((rows, bins, half), BF, True)],
        (embedding, w_left.T, w_right.T, flags),
    )
    received = exchange(send, "rows")
    share, received = lax.optimization_barrier((share, received))
    emb_all = exchange(share, "rows")
    predicted, send = call(
        tile_kernel,
        [((tile, tile), BF, False), ((devices, part + GROUP, tile), BF, True)],
        (offsets, near(left), near(received), flags, target.reshape(tile, tile), w_in, w_out.T, head_row, dist_bias.T),
        smem(),
        [
            ((tile, tile), F32),
            ((2, GROUP, hidden, tile), BF),
            ((2, GROUP, hidden, tile), F32),
            ((tile, tile), F32),
            ((tile, tile), F32),
            ((hidden, tile), F32),
            ((2, hidden, 2 * GROUP * tile), BF),
            ((2 * GROUP * tile, tile), BF),
            ((tile // GROUP, hidden, tile), F32),
            ((tile, 1), F32),
            ((tile, 1), F32),
        ],
    )
    send, emb_all = lax.optimization_barrier((send, emb_all))
    partial = exchange(send, ("rows", "band"))
    (send,) = call(functools.partial(total_kernel, owners), [(partial.shape, BF, True)], (near(partial),))
    complete = exchange(send, ("rows", "band"))
    mine, grad_embedding, grad_in, grad_out, grad_head, grad_bias = call(
        finish_kernel,
        [
            ((2 * channels, half), F32, True),
            ((bins, features // bands), BF, False),
            ((channels, hidden), F32, False),
            ((channels, hidden), F32, False),
            ((1, channels), F32, False),
            (dist_bias.shape[::-1], F32, False),
        ],
        (near(complete), near(emb_all), w_left.T, w_right.T, head_row),
    )
    other = lax.ppermute(mine, "band", [(source, source ^ 1) for source in range(bands)])
    grad_left, grad_right = call(arrange_kernel, [((channels, features), F32, False)] * 2, (near(mine), near(other)))
    return (
        predicted.reshape(target.shape),
        grad_embedding,
        grad_left.T,
        grad_right.T,
        grad_in,
        grad_out.T,
        grad_head.reshape(channels),
        grad_bias.T,
    )


def solution(mesh):
    placed = (
        P("rows", None),
        P(),
        P(),
        P(),
        P(),
        P(),
        P(),
        P("rows", "band"),
        P("rows"),
        P("rows", "band", None, None),
    )

    return jax.shard_map(
        on_device,
        mesh=mesh,
        in_specs=placed,
        out_specs=(P("rows", "band", None, None), P("rows", "band"), P(), P(), P(), P(), P(), P()),
        check_vma=False,
    )
```

```python
import functools
import math

import jax
import jax.numpy as jnp
from jax import lax
from jax.experimental import pallas as pl
from jax.experimental.pallas import tpu as pltpu
from jax.sharding import PartitionSpec as P


BF = jnp.bfloat16
F32 = jnp.float32
CURVE = math.sqrt(2.0 / math.pi)
STRETCH = (0.044715 * CURVE) ** (1.0 / 3.0)
LINEAR = CURVE / STRETCH
GROUP = 8
HALVES = 2
SMALL = 1 << 20
NT = (((1,), (1,)), ((), ()))
NN = (((1,), (0,)), ((), ()))


def mm(a, b, dims=NN):
    return lax.dot_general(a, b, dims, preferred_element_type=F32)


def split(x):
    high = x.astype(BF)
    return high, (x - high.astype(F32)).astype(BF)


def mm_wide(a, b, dims=NN):
    high, low = split(b)
    return mm(a, high, dims) + mm(a, low, dims)


def eye(count):
    return lax.broadcasted_iota(jnp.int32, (count, count), 0) == lax.broadcasted_iota(
        jnp.int32, (count, count), 1
    )


def to_col(row):
    count = row.shape[1]
    return jnp.sum(jnp.where(eye(count), jnp.broadcast_to(row, (count, count)), 0.0), axis=1, keepdims=True)


def to_row(col):
    count = col.shape[0]
    return jnp.sum(jnp.where(eye(count), jnp.broadcast_to(col, (count, count)), 0.0), axis=0, keepdims=True)


def project_kernel(emb_ref, wl_ref, wr_ref, flags_ref, left_ref, send_ref, share_ref):
    emb = emb_ref[...]
    bins = emb.shape[0]
    left_ref[...] = mm(wl_ref[...], emb, NT).astype(BF)
    flags = jnp.broadcast_to(flags_ref[...].astype(F32), (GROUP, bins))
    send_ref[...] = jnp.concatenate([mm(wr_ref[...], emb, NT), flags], axis=0).astype(BF)
    width = share_ref.shape[2]
    start = pl.multiple_of(lax.rem(lax.axis_index("band"), HALVES) * width, width)
    share = emb_ref[:, pl.ds(start, width)]

    def body(row, carry):
        share_ref[row] = share
        return carry

    lax.fori_loop(0, share_ref.shape[0], body, 0, unroll=share_ref.shape[0] <= 8)


def tile_kernel(
    offset_ref,
    left_ref,
    ahead_refs,
    flags_ref,
    target_ref,
    w_in_ref,
    w_out_ref,
    w_head_ref,
    bias_ref,
    pred_ref,
    send_ref,
    target_wide,
    act_ref,
    slope_ref,
    logit_ref,
    res_ref,
    col_ref,
    act_sum_ref,
    sums_ref,
    logit_col_ref,
    flag_col_ref,
):
    channels, hidden = w_in_ref.shape
    tile = target_ref.shape[0]
    noff = bias_ref.shape[0]
    rows, bands = lax.axis_size("rows"), lax.axis_size("band")
    part = 2 * channels // bands
    here, offset = lax.axis_index("rows"), offset_ref[0, 0]
    there = here + offset
    piece = ahead_refs[0][...].astype(F32)
    for step in range(1, noff):
        piece = jnp.where(offset == step, ahead_refs[step][...].astype(F32), piece)
    right = piece[:channels]
    col_flags = piece[channels : channels + 1] * (1.0 / (noff * tile))
    left = left_ref[...].astype(F32)
    off_row = lax.broadcasted_iota(jnp.int32, (noff, channels), 0)
    bias = to_col(jnp.sum(jnp.where(off_row == offset, bias_ref[...], 0.0), axis=0, keepdims=True))
    head_row = w_head_ref[...]
    head = to_col(head_row)
    w_out_t = w_out_ref[...].astype(F32)
    gain_row = jnp.sum(w_out_t * head, axis=0, keepdims=True)
    gain = to_col(gain_row) * 0.5
    gain_row = gain_row * (0.5 / STRETCH)
    logit_col_ref[...] = to_col(jnp.sum((left + bias) * head, axis=0, keepdims=True))
    logit_row = jnp.sum(right * head, axis=0, keepdims=True)
    flag_col_ref[...] = to_col(flags_ref[...].astype(F32))
    target_wide[...] = target_ref[...].astype(F32)
    shifted = right + bias
    w_in = w_in_ref[...]
    w_high, w_low = split(w_in.astype(F32).T * STRETCH)
    w_both = jnp.concatenate([w_high, w_low], axis=1)
    gain_high = gain_row.astype(BF).astype(F32)
    gain_low = gain_row - gain_high
    group_row = lax.broadcasted_iota(jnp.int32, (GROUP, 1), 0)
    gain_parts = [
        jnp.concatenate([jnp.where(group_row == step, piece, 0.0) for piece in (gain_high, gain_low)], axis=0).astype(BF)
        for step in range(GROUP)
    ]
    col_ref[...] = jnp.zeros_like(col_ref)
    act_sum_ref[...] = jnp.zeros_like(act_sum_ref)
    groups = tile // GROUP

    def start_of(group):
        return pl.multiple_of(group * GROUP, GROUP)

    def turn(group):
        return pltpu.roll(left, lax.rem(tile - start_of(group), tile), 1)

    def forward(turned, step, slot, logits):
        pair_in = (turned[:, step : step + 1] + shifted).astype(BF)
        x = mm(w_both, jnp.concatenate([pair_in, pair_in], axis=0))
        square = x * x
        inner = square + LINEAR
        bend = jnp.tanh(x * inner)
        lift = 1.0 + bend
        act = x * lift
        slope_ref[slot, step] = lift + (act * (1.0 - bend)) * (inner + (square + square))
        act = act.astype(BF)
        act_ref[slot, step] = act
        return logits + mm(gain_parts[step], act)

    def settle(group, logits):
        at = pl.ds(start_of(group), GROUP)
        logits = logits[:GROUP] + logits[GROUP:]
        logits = logits + logit_col_ref[at, :] + logit_row
        logit_ref[at, :] = logits
        res_ref[at, :] = flag_col_ref[at, :] * col_flags * (logits - target_wide[at, :])

    def backward(res, res_low, step, slot, group, total, acts):
        product = slope_ref[slot, step] * res[step : step + 1]
        sums_ref[group, :, step : step + 1] = jnp.sum(product, axis=1, keepdims=True)
        weighted = act_ref[slot, step] * res_low[step : step + 1]
        return total + product, acts + weighted.astype(F32)

    def none():
        return jnp.zeros((2 * GROUP, tile), F32)

    logits = none()
    turned = turn(0)
    for step in range(GROUP):
        logits = forward(turned, step, 0, logits)
    settle(0, logits)

    def body(index, carry):
        for slot in range(2):
            group = 2 * index + slot
            following = lax.rem(group + 1, groups)
            at = pl.ds(start_of(group), GROUP)
            res = res_ref[at, :]
            res_low = res.astype(BF)
            total, acts = col_ref[...], act_sum_ref[...]
            turned = turn(following)
            logits = none()
            for step in range(GROUP):
                logits = forward(turned, step, 1 - slot, logits)
                total, acts = backward(res, res_low, step, slot, group, total, acts)
            col_ref[...] = total
            act_sum_ref[...] = acts
            settle(following, logits)
        return carry

    lax.fori_loop(0, groups // 2, body, 0)

    pred_ref[...] = logit_ref[...].astype(BF)
    res = res_ref[...]
    res_col = jnp.sum(res, axis=0, keepdims=True)
    res_row = to_row(jnp.sum(res, axis=1, keepdims=True))
    res_all = jnp.sum(res_row, axis=1, keepdims=True)
    row_sum = jnp.zeros((hidden, tile), F32)
    lane = lax.broadcasted_iota(jnp.int32, (hidden, tile), 1)
    for group in range(groups):
        sums = sums_ref[group]
        row_sum = jnp.where(lane // GROUP == group, pltpu.roll(sums, group * GROUP, 1) if group else sums, row_sum)
    row_part = row_sum * gain
    act_sum = to_row(jnp.sum(act_sum_ref[...], axis=1, keepdims=True) * (0.5 / STRETCH))
    col_part = col_ref[...] * gain
    row_sums = head * res_row + mm_wide(w_in, row_part)
    col_sums = head * res_col + mm_wide(w_in, col_part)
    left_low, right_low = left_ref[...], right.astype(BF)
    in_term = (
        mm_wide(left_low, row_part, NT) + mm_wide(right_low, col_part, NT) + bias * to_row(jnp.sum(row_part, axis=1, keepdims=True))
    )
    head_term = jnp.sum(left * res_row + right * res_col + w_out_t * act_sum, axis=1, keepdims=True) + bias * res_all
    bias_sum = jnp.sum(row_sums, axis=1, keepdims=True)
    wide = jnp.zeros((channels, hidden), F32)
    lane = lax.broadcasted_iota(jnp.int32, (channels, hidden), 1)
    wide = jnp.where(lane == 1, head_term, wide)
    wide = jnp.where(lane == offset + 2, bias_sum, wide)
    flat = jnp.concatenate([wide] + [jnp.zeros_like(wide)] * (hidden // channels - 1), axis=0).T
    first = lax.broadcasted_iota(jnp.int32, (GROUP, hidden), 0) == 0
    small = jnp.concatenate([in_term, jnp.where(first, act_sum, flat[:GROUP])], axis=0)
    small_high = small.astype(BF).astype(F32)
    small_low = small - small_high
    owners = small.shape[0] // GROUP
    send_ref[...] = jnp.zeros_like(send_ref)
    for piece_index in range(3 * owners):
        source = small_low if piece_index // owners == 1 else small_high
        block = piece_index % owners
        send_ref[piece_index, part:, :] = source[block * GROUP : (block + 1) * GROUP].astype(BF)
    for quarter in range(bands // 2):
        send_ref[here * bands + quarter, :part, :] = row_sums[quarter * part : (quarter + 1) * part].astype(BF)

    @pl.when(there < rows)
    def _():
        for quarter in range(bands // 2):
            send_ref[there * bands + bands // 2 + quarter, :part, :] = col_sums[
                quarter * part : (quarter + 1) * part
            ].astype(BF)


def total_kernel(owners, recv_ref, send_ref):
    _, height, width = recv_ref.shape
    total = jnp.sum(recv_ref[...].astype(F32), axis=0)
    index = lax.axis_index("rows") * lax.axis_size("band") + lax.axis_index("band")
    low = total - total.astype(BF).astype(F32)
    row = lax.broadcasted_iota(jnp.int32, (height, width), 0)
    third = jnp.logical_and(index >= 2 * owners, index < 3 * owners)
    use_low = jnp.logical_and(third, row >= height - GROUP)
    send_ref[...] = jnp.broadcast_to(jnp.where(use_low, low, total).astype(BF)[None], send_ref.shape)


def finish_kernel(
    recv_ref, emb_ref, wl_ref, wr_ref, w_head_ref, share_ref, grad_emb_ref, in_ref, out_ref, head_ref, bias_ref
):
    rows = emb_ref.shape[0]
    devices, height, width = recv_ref.shape
    bands = devices // rows
    part = height - GROUP
    channels = in_ref.shape[0]

    def grads(row):
        return jnp.concatenate([recv_ref[row * bands + band, :part, :].astype(F32) for band in range(bands)], axis=0)

    def body(row, total):
        return total + mm(grads(row).astype(BF), emb_ref[row])

    share_ref[...] = lax.fori_loop(0, rows, body, jnp.zeros(share_ref.shape, F32), unroll=rows <= 8)
    own = grads(lax.axis_index("rows")).T.astype(BF)
    share = pl.ds(pl.multiple_of(lax.axis_index("band") * width, width), width)
    weights = jnp.concatenate([wl_ref[:, share], wr_ref[:, share]], axis=0)
    grad_emb_ref[...] = mm(own, weights).astype(BF)
    owners = channels // GROUP + 1
    small = [
        recv_ref[block, part:, :].astype(F32)
        + recv_ref[owners + block, part:, :].astype(F32)
        + recv_ref[2 * owners + block, part:, :].astype(F32)
        for block in range(owners)
    ]
    in_ref[...] = jnp.concatenate(small[:-1], axis=0)
    last = small[-1]
    out_ref[...] = last[:1] * to_col(w_head_ref[...])
    head_ref[...] = last[1:2, :channels]
    bias_ref[...] = last[2 : 2 + bias_ref.shape[0], :channels]


def arrange_kernel(own_ref, other_ref, left_ref, right_ref):
    channels = left_ref.shape[0]
    width = own_ref.shape[1]
    half = lax.rem(lax.axis_index("band"), HALVES)
    for ref, index in ((own_ref, half), (other_ref, 1 - half)):
        place = pl.ds(pl.multiple_of(index * width, width), width)
        left_ref[:, place] = ref[:channels]
        right_ref[:, place] = ref[channels:]


def vmem():
    return pl.BlockSpec(memory_space=pltpu.VMEM)


def smem():
    return pl.BlockSpec(memory_space=pltpu.SMEM)


def fits(shape, kind):
    return math.prod(shape) * jnp.dtype(kind).itemsize <= SMALL


def near(value):
    return pltpu.with_memory_space_constraint(value, pltpu.VMEM) if fits(value.shape, value.dtype) else value


def call(kernel, outs, args, first=None, scratch=()):
    return pl.pallas_call(
        kernel,
        out_shape=[
            pltpu.VMEM(shape, kind) if inner and fits(shape, kind) else jax.ShapeDtypeStruct(shape, kind) for shape, kind, inner in outs
        ],
        in_specs=[first or vmem()] + [jax.tree.map(lambda _: vmem(), arg) for arg in args[1:]],
        out_specs=[vmem()] * len(outs),
        scratch_shapes=[pltpu.VMEM(shape, kind) for shape, kind in scratch],
    )(*args)


def exchange(value, axes):
    return lax.all_to_all(value, axes, 0, 0, tiled=True)


def on_device(embedding, w_left, w_right, w_in, w_out, w_head, dist_bias, offsets, valid_bins, target):
    rows, bands = lax.axis_size("rows"), lax.axis_size("band")
    devices = rows * bands
    bins, features = embedding.shape
    channels, hidden = w_in.shape
    tile = target.shape[-1]
    part = 2 * channels // bands
    owners = channels // GROUP + 1
    noff = dist_bias.shape[1]
    half = features // HALVES
    flags = valid_bins.reshape(1, bins)
    head_row = w_head.reshape(1, channels)

    left, send, share = call(
        project_kernel,
        [((channels, bins), BF, True), ((channels + GROUP, bins), BF, True), ((rows, bins, half), BF, True)],
        (embedding, w_left.T, w_right.T, flags),
    )
    ahead = [send]
    for step in range(1, noff):
        ahead.append(lax.ppermute(send, "rows", [(source, source - step) for source in range(step, rows)]))
    emb_all = exchange(share, "rows")
    predicted, send = call(
        tile_kernel,
        [((tile, tile), BF, False), ((devices, part + GROUP, tile), BF, True)],
        (offsets, near(left), [near(piece) for piece in ahead], flags, target.reshape(tile, tile), w_in, w_out.T, head_row, dist_bias.T),
        smem(),
        [
            ((tile, tile), F32),
            ((2, GROUP, hidden, tile), BF),
            ((2, GROUP, hidden, tile), F32),
            ((tile, tile), F32),
            ((tile, tile), F32),
            ((hidden, tile), F32),
            ((hidden, tile), F32),
            ((tile // GROUP, hidden, tile), F32),
            ((tile, 1), F32),
            ((tile, 1), F32),
        ],
    )
    send, emb_all = lax.optimization_barrier((send, emb_all))
    partial = exchange(send, ("rows", "band"))
    (send,) = call(functools.partial(total_kernel, owners), [(partial.shape, BF, True)], (near(partial),))
    complete = exchange(send, ("rows", "band"))
    mine, grad_embedding, grad_in, grad_out, grad_head, grad_bias = call(
        finish_kernel,
        [
            ((2 * channels, half), F32, True),
            ((bins, features // bands), BF, False),
            ((channels, hidden), F32, False),
            ((channels, hidden), F32, False),
            ((1, channels), F32, False),
            (dist_bias.shape[::-1], F32, False),
        ],
        (near(complete), near(emb_all), w_left.T, w_right.T, head_row),
    )
    other = lax.ppermute(mine, "band", [(source, source ^ 1) for source in range(bands)])
    grad_left, grad_right = call(arrange_kernel, [((channels, features), F32, False)] * 2, (near(mine), near(other)))
    return (
        predicted.reshape(target.shape),
        grad_embedding,
        grad_left.T,
        grad_right.T,
        grad_in,
        grad_out.T,
        grad_head.reshape(channels),
        grad_bias.T,
    )


def solution(mesh):
    placed = (
        P("rows", None),
        P(),
        P(),
        P(),
        P(),
        P(),
        P(),
        P("rows", "band"),
        P("rows"),
        P("rows", "band", None, None),
    )

    return jax.shard_map(
        on_device,
        mesh=mesh,
        in_specs=placed,
        out_specs=(P("rows", "band", None, None), P("rows", "band"), P(), P(), P(), P(), P(), P()),
        check_vma=False,
    )
```

```python
import functools
import math

import jax
import jax.numpy as jnp
from jax import lax
from jax.experimental import pallas as pl
from jax.experimental.pallas import tpu as pltpu
from jax.sharding import PartitionSpec as P


BF = jnp.bfloat16
F32 = jnp.float32
CURVE = math.sqrt(2.0 / math.pi)
STRETCH = (0.044715 * CURVE) ** (1.0 / 3.0)
LINEAR = CURVE / STRETCH
GROUP = 8
UNROLL = 4
HALVES = 2
SMALL = 1 << 20
NT = (((1,), (1,)), ((), ()))
NN = (((1,), (0,)), ((), ()))


def mm(a, b, dims=NN):
    return lax.dot_general(a, b, dims, preferred_element_type=F32)


def split(x):
    high = x.astype(BF)
    return high, (x - high.astype(F32)).astype(BF)


def mm_wide(a, b, dims=NN):
    high, low = split(b)
    return mm(a, high, dims) + mm(a, low, dims)


def eye(count):
    return lax.broadcasted_iota(jnp.int32, (count, count), 0) == lax.broadcasted_iota(
        jnp.int32, (count, count), 1
    )


def to_col(row):
    count = row.shape[1]
    return jnp.sum(jnp.where(eye(count), jnp.broadcast_to(row, (count, count)), 0.0), axis=1, keepdims=True)


def to_row(col):
    count = col.shape[0]
    return jnp.sum(jnp.where(eye(count), jnp.broadcast_to(col, (count, count)), 0.0), axis=0, keepdims=True)


def project_kernel(emb_ref, wl_ref, wr_ref, flags_ref, left_ref, send_ref, share_ref):
    emb = emb_ref[...]
    bins = emb.shape[0]
    left_ref[...] = mm(wl_ref[...], emb, NT).astype(BF)
    flags = jnp.broadcast_to(flags_ref[...].astype(F32), (GROUP, bins))
    send_ref[...] = jnp.concatenate([mm(wr_ref[...], emb, NT), flags], axis=0).astype(BF)
    width = share_ref.shape[2]
    band, sides = lax.axis_index("band"), lax.axis_size("band") // HALVES
    start = pl.multiple_of((lax.rem(band, HALVES) * sides + band // HALVES) * width, width)
    share = emb_ref[:, pl.ds(start, width)]

    def body(row, carry):
        share_ref[row] = share
        return carry

    lax.fori_loop(0, share_ref.shape[0], body, 0, unroll=share_ref.shape[0] <= 8)


def tile_kernel(
    offset_ref,
    left_ref,
    ahead_refs,
    flags_ref,
    target_ref,
    w_in_ref,
    w_out_ref,
    w_head_ref,
    bias_ref,
    pred_ref,
    send_ref,
    target_wide,
    act_ref,
    slope_ref,
    pair_ref,
    logit_ref,
    res_ref,
    col_ref,
    act_sum_ref,
    sums_ref,
    logit_col_ref,
    flag_col_ref,
):
    channels, hidden = w_in_ref.shape
    tile = target_ref.shape[0]
    noff = bias_ref.shape[0]
    rows, bands = lax.axis_size("rows"), lax.axis_size("band")
    part = 2 * channels // bands
    here, offset = lax.axis_index("rows"), offset_ref[0, 0]
    there = here + offset
    piece = ahead_refs[0][...].astype(F32)
    for step in range(1, noff):
        piece = jnp.where(offset == step, ahead_refs[step][...].astype(F32), piece)
    right = piece[:channels]
    col_flags = piece[channels : channels + 1] * (1.0 / (noff * tile))
    left = left_ref[...].astype(F32)
    off_row = lax.broadcasted_iota(jnp.int32, (noff, channels), 0)
    bias = to_col(jnp.sum(jnp.where(off_row == offset, bias_ref[...], 0.0), axis=0, keepdims=True))
    head_row = w_head_ref[...]
    head = to_col(head_row)
    w_out_t = w_out_ref[...].astype(F32)
    gain_row = jnp.sum(w_out_t * head, axis=0, keepdims=True)
    gain = to_col(gain_row) * 0.5
    gain_row = gain_row * (0.5 / STRETCH)
    logit_col_ref[...] = to_col(jnp.sum((left + bias) * head, axis=0, keepdims=True))
    logit_row = jnp.sum(right * head, axis=0, keepdims=True)
    flag_col_ref[...] = to_col(flags_ref[...].astype(F32))
    target_wide[...] = target_ref[...].astype(F32)
    shifted = right + bias
    w_in = w_in_ref[...]
    w_high, w_low = split(w_in.astype(F32).T * STRETCH)
    w_both = jnp.concatenate([w_high, w_low], axis=1)
    gain_high = gain_row.astype(BF).astype(F32)
    gain_low = gain_row - gain_high
    group_row = lax.broadcasted_iota(jnp.int32, (GROUP, 1), 0)
    gain_parts = [
        jnp.concatenate([jnp.where(group_row == step, piece, 0.0) for piece in (gain_high, gain_low)], axis=0).astype(BF)
        for step in range(GROUP)
    ]
    col_ref[...] = jnp.zeros_like(col_ref)
    act_sum_ref[...] = jnp.zeros_like(act_sum_ref)
    groups = tile // GROUP

    def start_of(group):
        return pl.multiple_of(group * GROUP, GROUP)

    def prepare(group, slot):
        turned = pltpu.roll(left, lax.rem(tile - start_of(group), tile), 1)
        for step in range(GROUP):
            pair_ref[slot, step] = (turned[:, step : step + 1] + shifted).astype(BF)

    def forward(step, slot, logits):
        pair_in = pair_ref[slot, step]
        x = mm(w_both, jnp.concatenate([pair_in, pair_in], axis=0))
        square = x * x
        inner = square + LINEAR
        bend = jnp.tanh(x * inner)
        lift = 1.0 + bend
        act = x * lift
        slope_ref[slot, step] = lift + (act * (1.0 - bend)) * (inner + (square + square))
        act_ref[slot, step] = act
        return logits + mm(gain_parts[step], act.astype(BF))

    def settle(group, logits):
        at = pl.ds(start_of(group), GROUP)
        logits = logits[:GROUP] + logits[GROUP:]
        logits = logits + logit_col_ref[at, :] + logit_row
        logit_ref[at, :] = logits
        res_ref[at, :] = flag_col_ref[at, :] * col_flags * (logits - target_wide[at, :])

    def backward(res, step, slot, group, total, acts):
        product = slope_ref[slot, step] * res[step : step + 1]
        sums_ref[group, :, step : step + 1] = jnp.sum(product, axis=1, keepdims=True)
        return total + product, acts + act_ref[slot, step] * res[step : step + 1]

    def none():
        return jnp.zeros((2 * GROUP, tile), F32)

    prepare(0, 0)
    prepare(1, 1)
    logits = none()
    for step in range(GROUP):
        logits = forward(step, 0, logits)
    settle(0, logits)

    def body(index, carry):
        for block in range(UNROLL):
            slot = block % 2
            group = UNROLL * index + block
            following = lax.rem(group + 1, groups)
            res = res_ref[pl.ds(start_of(group), GROUP), :]
            total, acts = col_ref[...], act_sum_ref[...]
            prepare(lax.rem(group + 2, groups), slot)
            logits = none()
            for step in range(GROUP):
                logits = forward(step, 1 - slot, logits)
                total, acts = backward(res, step, slot, group, total, acts)
            col_ref[...] = total
            act_sum_ref[...] = acts
            settle(following, logits)
        return carry

    lax.fori_loop(0, groups // UNROLL, body, 0)

    pred_ref[...] = logit_ref[...].astype(BF)
    res = res_ref[...]
    res_col = jnp.sum(res, axis=0, keepdims=True)
    res_row = to_row(jnp.sum(res, axis=1, keepdims=True))
    res_all = jnp.sum(res_row, axis=1, keepdims=True)
    row_sum = jnp.zeros((hidden, tile), F32)
    lane = lax.broadcasted_iota(jnp.int32, (hidden, tile), 1)
    for group in range(groups):
        sums = sums_ref[group]
        row_sum = jnp.where(lane // GROUP == group, pltpu.roll(sums, group * GROUP, 1) if group else sums, row_sum)
    row_part = row_sum * gain
    act_sum = to_row(jnp.sum(act_sum_ref[...], axis=1, keepdims=True) * (0.5 / STRETCH))
    col_part = col_ref[...] * gain
    row_sums = head * res_row + mm_wide(w_in, row_part)
    col_sums = head * res_col + mm_wide(w_in, col_part)
    left_low, right_low = left_ref[...], right.astype(BF)
    in_term = (
        mm_wide(left_low, row_part, NT) + mm_wide(right_low, col_part, NT) + bias * to_row(jnp.sum(row_part, axis=1, keepdims=True))
    )
    head_term = jnp.sum(left * res_row + right * res_col + w_out_t * act_sum, axis=1, keepdims=True) + bias * res_all
    bias_sum = jnp.sum(row_sums, axis=1, keepdims=True)
    wide = jnp.zeros((channels, hidden), F32)
    lane = lax.broadcasted_iota(jnp.int32, (channels, hidden), 1)
    wide = jnp.where(lane == 1, head_term, wide)
    wide = jnp.where(lane == offset + 2, bias_sum, wide)
    flat = jnp.concatenate([wide] + [jnp.zeros_like(wide)] * (hidden // channels - 1), axis=0).T
    first = lax.broadcasted_iota(jnp.int32, (GROUP, hidden), 0) == 0
    small = jnp.concatenate([in_term, jnp.where(first, act_sum, flat[:GROUP])], axis=0)
    small_high = small.astype(BF).astype(F32)
    small_low = small - small_high
    owners = small.shape[0] // GROUP
    send_ref[...] = jnp.zeros_like(send_ref)
    for piece_index in range(3 * owners):
        source = small_low if piece_index // owners == 1 else small_high
        block = piece_index % owners
        send_ref[piece_index, part:, :] = source[block * GROUP : (block + 1) * GROUP].astype(BF)
    for quarter in range(bands // 2):
        send_ref[here * bands + quarter, :part, :] = row_sums[quarter * part : (quarter + 1) * part].astype(BF)

    @pl.when(there < rows)
    def _():
        for quarter in range(bands // 2):
            send_ref[there * bands + bands // 2 + quarter, :part, :] = col_sums[
                quarter * part : (quarter + 1) * part
            ].astype(BF)


def total_kernel(owners, recv_ref, send_ref):
    _, height, width = recv_ref.shape
    total = jnp.sum(recv_ref[...].astype(F32), axis=0)
    index = lax.axis_index("rows") * lax.axis_size("band") + lax.axis_index("band")
    low = total - total.astype(BF).astype(F32)
    row = lax.broadcasted_iota(jnp.int32, (height, width), 0)
    third = jnp.logical_and(index >= 2 * owners, index < 3 * owners)
    use_low = jnp.logical_and(third, row >= height - GROUP)
    send_ref[...] = jnp.broadcast_to(jnp.where(use_low, low, total).astype(BF)[None], send_ref.shape)


def grads_of(recv_ref, row, part):
    bands = lax.axis_size("band")
    return jnp.concatenate([recv_ref[row * bands + band, :part, :].astype(F32) for band in range(bands)], axis=0)


def share_kernel(recv_ref, near_ref, far_ref, share_ref):
    rows, width = near_ref.shape[0], near_ref.shape[2]
    part = recv_ref.shape[1] - GROUP
    side = lax.axis_index("band") // HALVES

    def body(row, totals):
        grads = grads_of(recv_ref, row, part).astype(BF)
        return totals[0] + mm(grads, near_ref[row]), totals[1] + mm(grads, far_ref[row])

    zero = jnp.zeros((share_ref.shape[0], width), F32)
    totals = lax.fori_loop(0, rows, body, (zero, zero), unroll=rows <= 8)
    for total, index in zip(totals, (side, 1 - side)):
        share_ref[:, pl.ds(pl.multiple_of(index * width, width), width)] = total


def finish_kernel(recv_ref, wl_ref, wr_ref, w_head_ref, grad_emb_ref, in_ref, out_ref, head_ref, bias_ref):
    _, height, width = recv_ref.shape
    part = height - GROUP
    channels = in_ref.shape[0]
    own = grads_of(recv_ref, lax.axis_index("rows"), part).T.astype(BF)
    share = pl.ds(pl.multiple_of(lax.axis_index("band") * width, width), width)
    weights = jnp.concatenate([wl_ref[:, share], wr_ref[:, share]], axis=0)
    grad_emb_ref[...] = mm(own, weights).astype(BF)
    owners = channels // GROUP + 1
    small = [
        recv_ref[block, part:, :].astype(F32)
        + recv_ref[owners + block, part:, :].astype(F32)
        + recv_ref[2 * owners + block, part:, :].astype(F32)
        for block in range(owners)
    ]
    in_ref[...] = jnp.concatenate(small[:-1], axis=0)
    last = small[-1]
    out_ref[...] = last[:1] * to_col(w_head_ref[...])
    head_ref[...] = last[1:2, :channels]
    bias_ref[...] = last[2 : 2 + bias_ref.shape[0], :channels]


def arrange_kernel(own_ref, other_ref, left_ref, right_ref):
    channels = left_ref.shape[0]
    width = own_ref.shape[1]
    half = lax.rem(lax.axis_index("band"), HALVES)
    for ref, index in ((own_ref, half), (other_ref, 1 - half)):
        place = pl.ds(pl.multiple_of(index * width, width), width)
        left_ref[:, place] = ref[:channels]
        right_ref[:, place] = ref[channels:]


def vmem():
    return pl.BlockSpec(memory_space=pltpu.VMEM)


def smem():
    return pl.BlockSpec(memory_space=pltpu.SMEM)


def fits(shape, kind):
    return math.prod(shape) * jnp.dtype(kind).itemsize <= SMALL


def near(value):
    return pltpu.with_memory_space_constraint(value, pltpu.VMEM) if fits(value.shape, value.dtype) else value


def call(kernel, outs, args, first=None, scratch=()):
    return pl.pallas_call(
        kernel,
        out_shape=[
            pltpu.VMEM(shape, kind) if inner and fits(shape, kind) else jax.ShapeDtypeStruct(shape, kind) for shape, kind, inner in outs
        ],
        in_specs=[first or vmem()] + [jax.tree.map(lambda _: vmem(), arg) for arg in args[1:]],
        out_specs=[vmem()] * len(outs),
        scratch_shapes=[pltpu.VMEM(shape, kind) for shape, kind in scratch],
    )(*args)


def exchange(value, axes):
    return lax.all_to_all(value, axes, 0, 0, tiled=True)


def on_device(embedding, w_left, w_right, w_in, w_out, w_head, dist_bias, offsets, valid_bins, target):
    rows, bands = lax.axis_size("rows"), lax.axis_size("band")
    devices = rows * bands
    bins, features = embedding.shape
    channels, hidden = w_in.shape
    tile = target.shape[-1]
    part = 2 * channels // bands
    owners = channels // GROUP + 1
    noff = dist_bias.shape[1]
    quarter = features // bands
    flags = valid_bins.reshape(1, bins)
    head_row = w_head.reshape(1, channels)

    left, send, share = call(
        project_kernel,
        [((channels, bins), BF, True), ((channels + GROUP, bins), BF, True), ((rows, bins, quarter), BF, True)],
        (embedding, w_left.T, w_right.T, flags),
    )
    ahead = [send]
    for step in range(1, noff):
        ahead.append(lax.ppermute(send, "rows", [(source, source - step) for source in range(step, rows)]))
    emb_all = exchange(share, "rows")
    predicted, send = call(
        tile_kernel,
        [((tile, tile), BF, True), ((devices, part + GROUP, tile), BF, True)],
        (offsets, near(left), [near(piece) for piece in ahead], near(flags), near(target.reshape(tile, tile)), near(w_in), near(w_out.T), near(head_row), near(dist_bias.T)),
        smem(),
        [
            ((tile, tile), F32),
            ((2, GROUP, hidden, tile), F32),
            ((2, GROUP, hidden, tile), F32),
            ((2, GROUP, channels, tile), BF),
            ((tile, tile), F32),
            ((tile, tile), F32),
            ((hidden, tile), F32),
            ((hidden, tile), F32),
            ((tile // GROUP, hidden, tile), F32),
            ((tile, 1), F32),
            ((tile, 1), F32),
        ],
    )
    send, emb_all = lax.optimization_barrier((send, emb_all))
    emb_far = lax.ppermute(emb_all, "band", [(source, source ^ HALVES) for source in range(bands)])
    partial = exchange(send, ("rows", "band"))
    (send,) = call(functools.partial(total_kernel, owners), [(partial.shape, BF, True)], (near(partial),))
    complete = exchange(send, ("rows", "band"))
    (mine,) = call(
        share_kernel, [((2 * channels, features // HALVES), F32, True)], (near(complete), near(emb_all), near(emb_far))
    )
    other = lax.ppermute(mine, "band", [(source, source ^ 1) for source in range(bands)])
    grad_embedding, grad_in, grad_out, grad_head, grad_bias = call(
        finish_kernel,
        [
            ((bins, features // bands), BF, False),
            ((channels, hidden), F32, False),
            ((channels, hidden), F32, False),
            ((1, channels), F32, False),
            (dist_bias.shape[::-1], F32, False),
        ],
        (near(complete), near(w_left.T), near(w_right.T), near(head_row)),
    )
    grad_left, grad_right = call(arrange_kernel, [((channels, features), F32, False)] * 2, (near(mine), near(other)))
    return (
        predicted.reshape(target.shape),
        grad_embedding,
        grad_left.T,
        grad_right.T,
        grad_in,
        grad_out.T,
        grad_head.reshape(channels),
        grad_bias.T,
    )


def solution(mesh):
    placed = (
        P("rows", None),
        P(),
        P(),
        P(),
        P(),
        P(),
        P(),
        P("rows", "band"),
        P("rows"),
        P("rows", "band", None, None),
    )

    return jax.shard_map(
        on_device,
        mesh=mesh,
        in_specs=placed,
        out_specs=(P("rows", "band", None, None), P("rows", "band"), P(), P(), P(), P(), P(), P()),
        check_vma=False,
    )
```

```python
import functools
import math

import jax
import jax.numpy as jnp
from jax import lax
from jax.experimental import pallas as pl
from jax.experimental.pallas import tpu as pltpu
from jax.sharding import PartitionSpec as P


BF = jnp.bfloat16
F32 = jnp.float32
CURVE = math.sqrt(2.0 / math.pi)
STRETCH = (0.044715 * CURVE) ** (1.0 / 3.0)
LINEAR = CURVE / STRETCH
GROUP = 8
UNROLL = 4
HALVES = 2
SMALL = 1 << 20
NT = (((1,), (1,)), ((), ()))
NN = (((1,), (0,)), ((), ()))


def mm(a, b, dims=NN):
    return lax.dot_general(a, b, dims, preferred_element_type=F32)


def split(x):
    high = x.astype(BF)
    return high, (x - high.astype(F32)).astype(BF)


def mm_wide(a, b, dims=NN):
    high, low = split(b)
    return mm(a, high, dims) + mm(a, low, dims)


def eye(count):
    return lax.broadcasted_iota(jnp.int32, (count, count), 0) == lax.broadcasted_iota(
        jnp.int32, (count, count), 1
    )


def to_col(row):
    count = row.shape[1]
    return jnp.sum(jnp.where(eye(count), jnp.broadcast_to(row, (count, count)), 0.0), axis=1, keepdims=True)


def to_row(col):
    count = col.shape[0]
    return jnp.sum(jnp.where(eye(count), jnp.broadcast_to(col, (count, count)), 0.0), axis=0, keepdims=True)


def project_kernel(
    offset_ref,
    emb_ref,
    wl_ref,
    wr_ref,
    flags_ref,
    target_ref,
    w_in_ref,
    w_out_ref,
    w_head_ref,
    bias_ref,
    left_ref,
    send_ref,
    share_ref,
    target_wide,
    w_both_ref,
    parts_ref,
    gain_ref,
    logit_col_ref,
    flag_col_ref,
    head_ref,
    own_bias_ref,
    weights_ref,
    w_in_near,
    w_out_near,
):
    emb = emb_ref[...]
    bins = emb.shape[0]
    left = mm(wl_ref[...], emb, NT).astype(BF)
    left_ref[...] = left
    flags_row = flags_ref[...].astype(F32)
    flags = jnp.broadcast_to(flags_row, (GROUP, bins))
    send_ref[...] = jnp.concatenate([mm(wr_ref[...], emb, NT), flags], axis=0).astype(BF)
    width = share_ref.shape[2]
    band, sides = lax.axis_index("band"), lax.axis_size("band") // HALVES
    start = pl.multiple_of((lax.rem(band, HALVES) * sides + band // HALVES) * width, width)
    share = emb_ref[:, pl.ds(start, width)]

    def body(row, carry):
        share_ref[row] = share
        return carry

    lax.fori_loop(0, share_ref.shape[0], body, 0, unroll=share_ref.shape[0] <= 8)
    target_wide[...] = target_ref[...].astype(F32)
    w_in = w_in_ref[...]
    w_in_near[...] = w_in
    w_out_near[...] = w_out_ref[...]
    w_high, w_low = split(w_in.astype(F32).T * STRETCH)
    w_both_ref[...] = jnp.concatenate([w_high, w_low], axis=1)
    head = to_col(w_head_ref[...])
    head_ref[...] = head
    off_row = lax.broadcasted_iota(jnp.int32, bias_ref.shape, 0)
    bias = to_col(jnp.sum(jnp.where(off_row == offset_ref[0, 0], bias_ref[...], 0.0), axis=0, keepdims=True))
    own_bias_ref[...] = bias
    gain_row = jnp.sum(w_out_ref[...].astype(F32) * head, axis=0, keepdims=True)
    gain_ref[...] = to_col(gain_row) * 0.5
    gain_row = gain_row * (0.5 / STRETCH)
    gain_high = gain_row.astype(BF).astype(F32)
    group_row = lax.broadcasted_iota(jnp.int32, (GROUP, 1), 0)
    for step in range(GROUP):
        parts_ref[step] = jnp.concatenate(
            [jnp.where(group_row == step, piece, 0.0) for piece in (gain_high, gain_row - gain_high)], axis=0
        ).astype(BF)
    logit_col_ref[...] = to_col(jnp.sum((left.astype(F32) + bias) * head, axis=0, keepdims=True))
    flag_col_ref[...] = to_col(flags_row)
    lanes = pl.ds(pl.multiple_of(band * width, width), width)
    weights_ref[...] = jnp.concatenate([wl_ref[:, lanes], wr_ref[:, lanes]], axis=0)


def tile_kernel(
    offset_ref,
    left_ref,
    ahead_refs,
    target_wide,
    w_both_ref,
    parts_ref,
    gain_ref,
    logit_col_ref,
    flag_col_ref,
    head_ref,
    own_bias_ref,
    w_in_ref,
    w_out_ref,
    pred_ref,
    send_ref,
    act_ref,
    slope_ref,
    pair_ref,
    logit_ref,
    res_ref,
    col_ref,
    act_sum_ref,
    sums_ref,
):
    channels, hidden = w_in_ref.shape
    tile = target_wide.shape[0]
    noff = len(ahead_refs)
    rows, bands = lax.axis_size("rows"), lax.axis_size("band")
    part = 2 * channels // bands
    here, offset = lax.axis_index("rows"), offset_ref[0, 0]
    there = here + offset
    piece = ahead_refs[0][...].astype(F32)
    for step in range(1, noff):
        piece = jnp.where(offset == step, ahead_refs[step][...].astype(F32), piece)
    right = piece[:channels]
    col_flags = piece[channels : channels + 1] * (1.0 / (noff * tile))
    left = left_ref[...].astype(F32)
    bias, head, gain = own_bias_ref[...], head_ref[...], gain_ref[...]
    logit_row = jnp.sum(right * head, axis=0, keepdims=True)
    shifted = right + bias
    w_both = w_both_ref[...]
    col_ref[...] = jnp.zeros_like(col_ref)
    act_sum_ref[...] = jnp.zeros_like(act_sum_ref)
    groups = tile // GROUP

    def start_of(group):
        return pl.multiple_of(group * GROUP, GROUP)

    def prepare(group, slot):
        turned = pltpu.roll(left, lax.rem(tile - start_of(group), tile), 1)
        for step in range(GROUP):
            pair_ref[slot, step] = (turned[:, step : step + 1] + shifted).astype(BF)

    def forward(step, slot, logits):
        pair_in = pair_ref[slot, step]
        x = mm(w_both, jnp.concatenate([pair_in, pair_in], axis=0))
        square = x * x
        inner = square + LINEAR
        bend = jnp.tanh(x * inner)
        lift = 1.0 + bend
        act = x * lift
        slope_ref[slot, step] = lift + (act * (1.0 - bend)) * (inner + (square + square))
        act_ref[slot, step] = act
        return logits + mm(parts_ref[step], act.astype(BF))

    def settle(group, logits):
        at = pl.ds(start_of(group), GROUP)
        logits = logits[:GROUP] + logits[GROUP:]
        logits = logits + logit_col_ref[at, :] + logit_row
        logit_ref[at, :] = logits
        res_ref[at, :] = flag_col_ref[at, :] * col_flags * (logits - target_wide[at, :])

    def backward(res, step, slot, group, total, acts):
        product = slope_ref[slot, step] * res[step : step + 1]
        sums_ref[group, :, step : step + 1] = jnp.sum(product, axis=1, keepdims=True)
        return total + product, acts + act_ref[slot, step] * res[step : step + 1]

    def none():
        return jnp.zeros((2 * GROUP, tile), F32)

    prepare(0, 0)
    prepare(1, 1)
    logits = none()
    for step in range(GROUP):
        logits = forward(step, 0, logits)
    settle(0, logits)

    def body(index, carry):
        for block in range(UNROLL):
            slot = block % 2
            group = UNROLL * index + block
            following = lax.rem(group + 1, groups)
            res = res_ref[pl.ds(start_of(group), GROUP), :]
            total, acts = col_ref[...], act_sum_ref[...]
            prepare(lax.rem(group + 2, groups), slot)
            logits = none()
            for step in range(GROUP):
                logits = forward(step, 1 - slot, logits)
                total, acts = backward(res, step, slot, group, total, acts)
            col_ref[...] = total
            act_sum_ref[...] = acts
            settle(following, logits)
        return carry

    lax.fori_loop(0, groups // UNROLL, body, 0)

    pred_ref[...] = logit_ref[...].astype(BF)
    res = res_ref[...]
    res_col = jnp.sum(res, axis=0, keepdims=True)
    res_row = to_row(jnp.sum(res, axis=1, keepdims=True))
    res_all = jnp.sum(res_row, axis=1, keepdims=True)
    row_sum = jnp.zeros((hidden, tile), F32)
    lane = lax.broadcasted_iota(jnp.int32, (hidden, tile), 1)
    for group in range(groups):
        sums = sums_ref[group]
        row_sum = jnp.where(lane // GROUP == group, pltpu.roll(sums, group * GROUP, 1) if group else sums, row_sum)
    row_part = row_sum * gain
    act_sum = to_row(jnp.sum(act_sum_ref[...], axis=1, keepdims=True) * (0.5 / STRETCH))
    col_part = col_ref[...] * gain
    w_in, w_out_t = w_in_ref[...], w_out_ref[...].astype(F32)
    row_sums = head * res_row + mm_wide(w_in, row_part)
    col_sums = head * res_col + mm_wide(w_in, col_part)
    left_low, right_low = left_ref[...], right.astype(BF)
    in_term = (
        mm_wide(left_low, row_part, NT) + mm_wide(right_low, col_part, NT) + bias * to_row(jnp.sum(row_part, axis=1, keepdims=True))
    )
    head_term = jnp.sum(left * res_row + right * res_col + w_out_t * act_sum, axis=1, keepdims=True) + bias * res_all
    bias_sum = jnp.sum(row_sums, axis=1, keepdims=True)
    wide = jnp.zeros((channels, hidden), F32)
    lane = lax.broadcasted_iota(jnp.int32, (channels, hidden), 1)
    wide = jnp.where(lane == 1, head_term, wide)
    wide = jnp.where(lane == offset + 2, bias_sum, wide)
    flat = jnp.concatenate([wide] + [jnp.zeros_like(wide)] * (hidden // channels - 1), axis=0).T
    first = lax.broadcasted_iota(jnp.int32, (GROUP, hidden), 0) == 0
    small = jnp.concatenate([in_term, jnp.where(first, act_sum, flat[:GROUP])], axis=0)
    small_high = small.astype(BF).astype(F32)
    small_low = small - small_high
    owners = small.shape[0] // GROUP
    send_ref[...] = jnp.zeros_like(send_ref)
    for piece_index in range(3 * owners):
        source = small_low if piece_index // owners == 1 else small_high
        block = piece_index % owners
        send_ref[piece_index, part:, :] = source[block * GROUP : (block + 1) * GROUP].astype(BF)
    for quarter in range(bands // 2):
        send_ref[here * bands + quarter, :part, :] = row_sums[quarter * part : (quarter + 1) * part].astype(BF)

    @pl.when(there < rows)
    def _():
        for quarter in range(bands // 2):
            send_ref[there * bands + bands // 2 + quarter, :part, :] = col_sums[
                quarter * part : (quarter + 1) * part
            ].astype(BF)


def total_kernel(owners, recv_ref, send_ref):
    _, height, width = recv_ref.shape
    total = jnp.sum(recv_ref[...].astype(F32), axis=0)
    index = lax.axis_index("rows") * lax.axis_size("band") + lax.axis_index("band")
    low = total - total.astype(BF).astype(F32)
    row = lax.broadcasted_iota(jnp.int32, (height, width), 0)
    third = jnp.logical_and(index >= 2 * owners, index < 3 * owners)
    use_low = jnp.logical_and(third, row >= height - GROUP)
    send_ref[...] = jnp.broadcast_to(jnp.where(use_low, low, total).astype(BF)[None], send_ref.shape)


def grads_of(recv_ref, row, part):
    bands = lax.axis_size("band")
    return jnp.concatenate([recv_ref[row * bands + band, :part, :].astype(F32) for band in range(bands)], axis=0)


def share_kernel(recv_ref, near_ref, far_ref, share_ref):
    rows, width = near_ref.shape[0], near_ref.shape[2]
    part = recv_ref.shape[1] - GROUP
    side = lax.axis_index("band") // HALVES

    def body(row, totals):
        grads = grads_of(recv_ref, row, part).astype(BF)
        return totals[0] + mm(grads, near_ref[row]), totals[1] + mm(grads, far_ref[row])

    zero = jnp.zeros((share_ref.shape[0], width), F32)
    totals = lax.fori_loop(0, rows, body, (zero, zero), unroll=rows <= 8)
    for total, index in zip(totals, (side, 1 - side)):
        share_ref[:, pl.ds(pl.multiple_of(index * width, width), width)] = total


def finish_kernel(recv_ref, weights_ref, head_ref_in, pred_near, pred_ref, grad_emb_ref, in_ref, out_ref, head_ref, bias_ref):
    _, height, _ = recv_ref.shape
    part = height - GROUP
    channels = in_ref.shape[0]
    own = grads_of(recv_ref, lax.axis_index("rows"), part).T.astype(BF)
    grad_emb_ref[...] = mm(own, weights_ref[...]).astype(BF)
    pred_ref[...] = pred_near[...]
    owners = channels // GROUP + 1
    small = [
        recv_ref[block, part:, :].astype(F32)
        + recv_ref[owners + block, part:, :].astype(F32)
        + recv_ref[2 * owners + block, part:, :].astype(F32)
        for block in range(owners)
    ]
    in_ref[...] = jnp.concatenate(small[:-1], axis=0)
    last = small[-1]
    out_ref[...] = last[:1] * head_ref_in[...]
    head_ref[...] = last[1:2, :channels]
    bias_ref[...] = last[2 : 2 + bias_ref.shape[0], :channels]


def arrange_kernel(own_ref, other_ref, left_ref, right_ref):
    channels = left_ref.shape[0]
    width = own_ref.shape[1]
    half = lax.rem(lax.axis_index("band"), HALVES)
    for ref, index in ((own_ref, half), (other_ref, 1 - half)):
        place = pl.ds(pl.multiple_of(index * width, width), width)
        left_ref[:, place] = ref[:channels]
        right_ref[:, place] = ref[channels:]


def vmem():
    return pl.BlockSpec(memory_space=pltpu.VMEM)


def smem():
    return pl.BlockSpec(memory_space=pltpu.SMEM)


def fits(shape, kind):
    return math.prod(shape) * jnp.dtype(kind).itemsize <= SMALL


def near(value):
    return pltpu.with_memory_space_constraint(value, pltpu.VMEM) if fits(value.shape, value.dtype) else value


def call(kernel, outs, args, first=None, scratch=()):
    return pl.pallas_call(
        kernel,
        out_shape=[
            pltpu.VMEM(shape, kind) if inner and fits(shape, kind) else jax.ShapeDtypeStruct(shape, kind) for shape, kind, inner in outs
        ],
        in_specs=[first or vmem()] + [jax.tree.map(lambda _: vmem(), arg) for arg in args[1:]],
        out_specs=[vmem()] * len(outs),
        scratch_shapes=[pltpu.VMEM(shape, kind) for shape, kind in scratch],
    )(*args)


def exchange(value, axes):
    return lax.all_to_all(value, axes, 0, 0, tiled=True)


def on_device(embedding, w_left, w_right, w_in, w_out, w_head, dist_bias, offsets, valid_bins, target):
    rows, bands = lax.axis_size("rows"), lax.axis_size("band")
    devices = rows * bands
    bins, features = embedding.shape
    channels, hidden = w_in.shape
    tile = target.shape[-1]
    part = 2 * channels // bands
    owners = channels // GROUP + 1
    noff = dist_bias.shape[1]
    quarter = features // bands
    flags = valid_bins.reshape(1, bins)

    (
        left,
        send,
        share,
        target_wide,
        w_both,
        parts,
        gain,
        logit_col,
        flag_col,
        head,
        bias,
        weights,
        w_in_near,
        w_out_near,
    ) = call(
        project_kernel,
        [
            ((channels, bins), BF, True),
            ((channels + GROUP, bins), BF, True),
            ((rows, bins, quarter), BF, True),
            ((tile, tile), F32, True),
            ((hidden, 2 * channels), BF, True),
            ((GROUP, 2 * GROUP, hidden), BF, True),
            ((hidden, 1), F32, True),
            ((tile, 1), F32, True),
            ((tile, 1), F32, True),
            ((channels, 1), F32, True),
            ((channels, 1), F32, True),
            ((2 * channels, quarter), BF, True),
            ((channels, hidden), BF, True),
            ((channels, hidden), BF, True),
        ],
        (
            offsets,
            embedding,
            w_left.T,
            w_right.T,
            flags,
            target.reshape(tile, tile),
            w_in,
            w_out.T,
            w_head.reshape(1, channels),
            dist_bias.T,
        ),
        smem(),
    )
    ahead = [send]
    for step in range(1, noff):
        ahead.append(lax.ppermute(send, "rows", [(source, source - step) for source in range(step, rows)]))
    emb_all = exchange(share, "rows")
    predicted, send = call(
        tile_kernel,
        [((tile, tile), BF, True), ((devices, part + GROUP, tile), BF, True)],
        (
            offsets,
            near(left),
            [near(piece) for piece in ahead],
            near(target_wide),
            near(w_both),
            near(parts),
            near(gain),
            near(logit_col),
            near(flag_col),
            near(head),
            near(bias),
            near(w_in_near),
            near(w_out_near),
        ),
        smem(),
        [
            ((2, GROUP, hidden, tile), F32),
            ((2, GROUP, hidden, tile), F32),
            ((2, GROUP, channels, tile), BF),
            ((tile, tile), F32),
            ((tile, tile), F32),
            ((hidden, tile), F32),
            ((hidden, tile), F32),
            ((tile // GROUP, hidden, tile), F32),
        ],
    )
    send, emb_all = lax.optimization_barrier((send, emb_all))
    emb_far = lax.ppermute(emb_all, "band", [(source, source ^ HALVES) for source in range(bands)])
    partial = exchange(send, ("rows", "band"))
    (send,) = call(functools.partial(total_kernel, owners), [(partial.shape, BF, True)], (near(partial),))
    send, emb_far = lax.optimization_barrier((send, emb_far))
    complete = exchange(send, ("rows", "band"))
    (mine,) = call(
        share_kernel, [((2 * channels, features // HALVES), F32, True)], (near(complete), near(emb_all), near(emb_far))
    )
    other = lax.ppermute(mine, "band", [(source, source ^ 1) for source in range(bands)])
    predicted, grad_embedding, grad_in, grad_out, grad_head, grad_bias = call(
        finish_kernel,
        [
            ((tile, tile), BF, False),
            ((bins, features // bands), BF, False),
            ((channels, hidden), F32, False),
            ((channels, hidden), F32, False),
            ((1, channels), F32, False),
            (dist_bias.shape[::-1], F32, False),
        ],
        (near(complete), near(weights), near(head), near(predicted)),
    )
    grad_left, grad_right = call(arrange_kernel, [((channels, features), F32, False)] * 2, (near(mine), near(other)))
    return (
        predicted.reshape(target.shape),
        grad_embedding,
        grad_left.T,
        grad_right.T,
        grad_in,
        grad_out.T,
        grad_head.reshape(channels),
        grad_bias.T,
    )


def solution(mesh):
    placed = (
        P("rows", None),
        P(),
        P(),
        P(),
        P(),
        P(),
        P(),
        P("rows", "band"),
        P("rows"),
        P("rows", "band", None, None),
    )

    return jax.shard_map(
        on_device,
        mesh=mesh,
        in_specs=placed,
        out_specs=(P("rows", "band", None, None), P("rows", "band"), P(), P(), P(), P(), P(), P()),
        check_vma=False,
    )
```

```python
import functools
import math

import jax
import jax.numpy as jnp
from jax import lax
from jax.experimental import pallas as pl
from jax.experimental.pallas import tpu as pltpu
from jax.sharding import PartitionSpec as P


BF = jnp.bfloat16
F32 = jnp.float32
CURVE = math.sqrt(2.0 / math.pi)
STRETCH = (0.044715 * CURVE) ** (1.0 / 3.0)
LINEAR = CURVE / STRETCH
GROUP = 8
UNROLL = 4
HALVES = 2
SMALL = 1 << 20
NT = (((1,), (1,)), ((), ()))
NN = (((1,), (0,)), ((), ()))


def mm(a, b, dims=NN):
    return lax.dot_general(a, b, dims, preferred_element_type=F32)


def split(x):
    high = x.astype(BF)
    return high, (x - high.astype(F32)).astype(BF)


def mm_wide(a, b, dims=NN):
    high, low = split(b)
    return mm(a, high, dims) + mm(a, low, dims)


def eye(count):
    return lax.broadcasted_iota(jnp.int32, (count, count), 0) == lax.broadcasted_iota(
        jnp.int32, (count, count), 1
    )


def to_col(row):
    count = row.shape[1]
    return jnp.sum(jnp.where(eye(count), jnp.broadcast_to(row, (count, count)), 0.0), axis=1, keepdims=True)


def to_row(col):
    count = col.shape[0]
    return jnp.sum(jnp.where(eye(count), jnp.broadcast_to(col, (count, count)), 0.0), axis=0, keepdims=True)


def project_kernel(
    offset_ref,
    emb_ref,
    wl_ref,
    wr_ref,
    flags_ref,
    target_ref,
    w_in_ref,
    w_out_ref,
    w_head_ref,
    bias_ref,
    left_ref,
    send_ref,
    share_ref,
    target_wide,
    w_both_ref,
    parts_ref,
    gain_ref,
    logit_col_ref,
    flag_col_ref,
    head_ref,
    own_bias_ref,
    weights_ref,
    w_in_near,
    w_out_near,
):
    emb = emb_ref[...]
    bins = emb.shape[0]
    left = mm(wl_ref[...], emb, NT).astype(BF)
    left_ref[...] = left
    flags_row = flags_ref[...].astype(F32)
    flags = jnp.broadcast_to(flags_row, (GROUP, bins))
    send_ref[...] = jnp.concatenate([mm(wr_ref[...], emb, NT), flags], axis=0).astype(BF)
    width = share_ref.shape[2]
    band, sides = lax.axis_index("band"), lax.axis_size("band") // HALVES
    start = pl.multiple_of((lax.rem(band, HALVES) * sides + band // HALVES) * width, width)
    share = emb_ref[:, pl.ds(start, width)]

    def body(row, carry):
        share_ref[row] = share
        return carry

    lax.fori_loop(0, share_ref.shape[0], body, 0, unroll=share_ref.shape[0] <= 8)
    target_wide[...] = target_ref[...].astype(F32)
    w_in = w_in_ref[...]
    w_in_near[...] = w_in
    w_out_near[...] = w_out_ref[...]
    w_high, w_low = split(w_in.astype(F32).T * STRETCH)
    w_both_ref[...] = jnp.concatenate([w_high, w_low], axis=1)
    head = to_col(w_head_ref[...])
    head_ref[...] = head
    off_row = lax.broadcasted_iota(jnp.int32, bias_ref.shape, 0)
    bias = to_col(jnp.sum(jnp.where(off_row == offset_ref[0, 0], bias_ref[...], 0.0), axis=0, keepdims=True))
    own_bias_ref[...] = bias
    gain_row = jnp.sum(w_out_ref[...].astype(F32) * head, axis=0, keepdims=True)
    gain_ref[...] = to_col(gain_row) * 0.5
    gain_row = gain_row * (0.5 / STRETCH)
    gain_high = gain_row.astype(BF).astype(F32)
    group_row = lax.broadcasted_iota(jnp.int32, (GROUP, 1), 0)
    for step in range(GROUP):
        parts_ref[step] = jnp.concatenate(
            [jnp.where(group_row == step, piece, 0.0) for piece in (gain_high, gain_row - gain_high)], axis=0
        ).astype(BF)
    logit_col_ref[...] = to_col(jnp.sum((left.astype(F32) + bias) * head, axis=0, keepdims=True))
    flag_col_ref[...] = to_col(flags_row)
    lanes = pl.ds(pl.multiple_of(band * width, width), width)
    weights_ref[...] = jnp.concatenate([wl_ref[:, lanes], wr_ref[:, lanes]], axis=0)


def tile_kernel(
    offset_ref,
    left_ref,
    ahead_refs,
    target_wide,
    w_both_ref,
    parts_ref,
    gain_ref,
    logit_col_ref,
    flag_col_ref,
    head_ref,
    own_bias_ref,
    w_in_ref,
    w_out_ref,
    pred_ref,
    send_ref,
    act_ref,
    slope_ref,
    pair_ref,
    logit_ref,
    res_ref,
    col_ref,
    act_sum_ref,
    sums_ref,
):
    channels, hidden = w_in_ref.shape
    tile = target_wide.shape[0]
    noff = len(ahead_refs)
    rows, bands = lax.axis_size("rows"), lax.axis_size("band")
    part = 2 * channels // bands
    here, offset = lax.axis_index("rows"), offset_ref[0, 0]
    there = here + offset
    piece = ahead_refs[0][...].astype(F32)
    for step in range(1, noff):
        piece = jnp.where(offset == step, ahead_refs[step][...].astype(F32), piece)
    right = piece[:channels]
    col_flags = piece[channels : channels + 1] * (1.0 / (noff * tile))
    left = left_ref[...].astype(F32)
    bias, head, gain = own_bias_ref[...], head_ref[...], gain_ref[...]
    logit_row = jnp.sum(right * head, axis=0, keepdims=True)
    shifted = right + bias
    w_both = w_both_ref[...]
    col_ref[...] = jnp.zeros_like(col_ref)
    act_sum_ref[...] = jnp.zeros_like(act_sum_ref)
    groups = tile // GROUP

    def start_of(group):
        return pl.multiple_of(group * GROUP, GROUP)

    def prepare(group, slot):
        turned = pltpu.roll(left, lax.rem(tile - start_of(group), tile), 1)
        for step in range(GROUP):
            pair_ref[slot, step] = (turned[:, step : step + 1] + shifted).astype(BF)

    def forward(step, slot, logits):
        pair_in = pair_ref[slot, step]
        x = mm(w_both, jnp.concatenate([pair_in, pair_in], axis=0))
        square = x * x
        inner = square + LINEAR
        bend = jnp.tanh(x * inner)
        lift = 1.0 + bend
        act = x * lift
        slope_ref[slot, step] = lift + (act * (1.0 - bend)) * (inner + (square + square))
        act_ref[slot, step] = act
        return logits + mm(parts_ref[step], act.astype(BF))

    def settle(group, logits):
        at = pl.ds(start_of(group), GROUP)
        logits = logits[:GROUP] + logits[GROUP:]
        logits = logits + logit_col_ref[at, :] + logit_row
        logit_ref[at, :] = logits
        res_ref[at, :] = flag_col_ref[at, :] * col_flags * (logits - target_wide[at, :])

    def backward(res, step, slot, group, total, acts):
        product = slope_ref[slot, step] * res[step : step + 1]
        sums_ref[group, :, step : step + 1] = jnp.sum(product, axis=1, keepdims=True)
        return total + product, acts + act_ref[slot, step] * res[step : step + 1]

    def none():
        return jnp.zeros((2 * GROUP, tile), F32)

    prepare(0, 0)
    prepare(1, 1)
    logits = none()
    for step in range(GROUP):
        logits = forward(step, 0, logits)
    settle(0, logits)

    def body(index, carry):
        for block in range(UNROLL):
            slot = block % 2
            group = UNROLL * index + block
            following = lax.rem(group + 1, groups)
            res = res_ref[pl.ds(start_of(group), GROUP), :]
            total, acts = col_ref[...], act_sum_ref[...]
            prepare(lax.rem(group + 2, groups), slot)
            logits = none()
            for step in range(GROUP):
                logits = forward(step, 1 - slot, logits)
                total, acts = backward(res, step, slot, group, total, acts)
            col_ref[...] = total
            act_sum_ref[...] = acts
            settle(following, logits)
        return carry

    lax.fori_loop(0, groups // UNROLL, body, 0)

    pred_ref[...] = logit_ref[...].astype(BF)
    res = res_ref[...]
    res_col = jnp.sum(res, axis=0, keepdims=True)
    res_row = to_row(jnp.sum(res, axis=1, keepdims=True))
    res_all = jnp.sum(res_row, axis=1, keepdims=True)
    row_sum = jnp.zeros((hidden, tile), F32)
    lane = lax.broadcasted_iota(jnp.int32, (hidden, tile), 1)
    for group in range(groups):
        sums = sums_ref[group]
        row_sum = jnp.where(lane // GROUP == group, pltpu.roll(sums, group * GROUP, 1) if group else sums, row_sum)
    row_part = row_sum * gain
    act_sum = to_row(jnp.sum(act_sum_ref[...], axis=1, keepdims=True) * (0.5 / STRETCH))
    col_part = col_ref[...] * gain
    w_in, w_out_t = w_in_ref[...], w_out_ref[...].astype(F32)
    row_sums = head * res_row + mm_wide(w_in, row_part)
    col_sums = head * res_col + mm_wide(w_in, col_part)
    left_low, right_low = left_ref[...], right.astype(BF)
    in_term = (
        mm_wide(left_low, row_part, NT) + mm_wide(right_low, col_part, NT) + bias * to_row(jnp.sum(row_part, axis=1, keepdims=True))
    )
    head_term = jnp.sum(left * res_row + right * res_col + w_out_t * act_sum, axis=1, keepdims=True) + bias * res_all
    bias_sum = jnp.sum(row_sums, axis=1, keepdims=True)
    wide = jnp.zeros((channels, hidden), F32)
    lane = lax.broadcasted_iota(jnp.int32, (channels, hidden), 1)
    wide = jnp.where(lane == 1, head_term, wide)
    wide = jnp.where(lane == offset + 2, bias_sum, wide)
    flat = jnp.concatenate([wide] + [jnp.zeros_like(wide)] * (hidden // channels - 1), axis=0).T
    first = lax.broadcasted_iota(jnp.int32, (GROUP, hidden), 0) == 0
    small = jnp.concatenate([in_term, jnp.where(first, act_sum, flat[:GROUP])], axis=0)
    small_high = small.astype(BF).astype(F32)
    small_low = small - small_high
    blocks = small.shape[0] // GROUP
    send_ref[...] = jnp.zeros_like(send_ref)
    for block in range(blocks):
        lines = slice(block * GROUP, (block + 1) * GROUP)
        piece = jnp.concatenate([small_high[lines], small_low[lines]], axis=0)
        for band in range(2):
            send_ref[block * bands + band] = piece.astype(BF)
        send_ref[spare_of(block, blocks, bands)] = jnp.where(here == block, piece, 0.0).astype(BF)
    for quarter in range(bands // 2):
        send_ref[here * bands + quarter] = row_sums[quarter * part : (quarter + 1) * part].astype(BF)

    @pl.when(there < rows)
    def _():
        for quarter in range(bands // 2):
            send_ref[there * bands + bands // 2 + quarter] = col_sums[quarter * part : (quarter + 1) * part].astype(BF)


def spare_of(block, blocks, bands):
    return (blocks + block // 2) * bands + block % 2


def total_kernel(blocks, recv_ref, send_ref):
    devices, part, width = recv_ref.shape
    bands = lax.axis_size("band")
    here, band = lax.axis_index("rows"), lax.axis_index("band")

    def body(row, totals):
        total = recv_ref[row * bands].astype(F32)
        for source in range(1, bands):
            total = total + recv_ref[row * bands + source].astype(F32)
        mine = jnp.where(row == here, total, 0.0)
        return totals[0] + mine, totals[1] + (total - mine)

    zero = jnp.zeros((part, width), F32)
    own, rest = lax.fori_loop(0, devices // bands, body, (zero, zero), unroll=devices // bands <= 8)
    grads = jnp.where(band < bands // 2, own, own + rest)
    small = rest[:GROUP] + rest[GROUP:]
    second = jnp.logical_and(band == 1, here < blocks)
    small = jnp.where(second, small - small.astype(BF).astype(F32), small)
    piece = jnp.concatenate([grads, small], axis=0).astype(BF)
    send_ref[...] = jnp.broadcast_to(piece[None], send_ref.shape)


def grads_of(recv_ref, row, part):
    bands = lax.axis_size("band")
    return jnp.concatenate([recv_ref[row * bands + band, :part, :].astype(F32) for band in range(bands)], axis=0)


def share_kernel(recv_ref, near_ref, far_ref, share_ref):
    rows, width = near_ref.shape[0], near_ref.shape[2]
    part = recv_ref.shape[1] - GROUP
    side = lax.axis_index("band") // HALVES

    def body(row, totals):
        grads = grads_of(recv_ref, row, part).astype(BF)
        return totals[0] + mm(grads, near_ref[row]), totals[1] + mm(grads, far_ref[row])

    zero = jnp.zeros((share_ref.shape[0], width), F32)
    totals = lax.fori_loop(0, rows, body, (zero, zero), unroll=rows <= 8)
    for total, index in zip(totals, (side, 1 - side)):
        share_ref[:, pl.ds(pl.multiple_of(index * width, width), width)] = total


def finish_kernel(recv_ref, weights_ref, head_ref_in, pred_near, pred_ref, grad_emb_ref, in_ref, out_ref, head_ref, bias_ref):
    _, height, _ = recv_ref.shape
    part = height - GROUP
    channels = in_ref.shape[0]
    own = grads_of(recv_ref, lax.axis_index("rows"), part).T.astype(BF)
    grad_emb_ref[...] = mm(own, weights_ref[...]).astype(BF)
    pred_ref[...] = pred_near[...]
    blocks = channels // GROUP + 1
    bands = lax.axis_size("band")
    small = [
        recv_ref[block * bands, part:, :].astype(F32)
        + recv_ref[block * bands + 1, part:, :].astype(F32)
        + recv_ref[spare_of(block, blocks, bands), part:, :].astype(F32)
        for block in range(blocks)
    ]
    in_ref[...] = jnp.concatenate(small[:-1], axis=0)
    last = small[-1]
    out_ref[...] = last[:1] * head_ref_in[...]
    head_ref[...] = last[1:2, :channels]
    bias_ref[...] = last[2 : 2 + bias_ref.shape[0], :channels]


def arrange_kernel(own_ref, other_ref, left_ref, right_ref):
    channels = left_ref.shape[0]
    width = own_ref.shape[1]
    half = lax.rem(lax.axis_index("band"), HALVES)
    for ref, index in ((own_ref, half), (other_ref, 1 - half)):
        place = pl.ds(pl.multiple_of(index * width, width), width)
        left_ref[:, place] = ref[:channels]
        right_ref[:, place] = ref[channels:]


def vmem():
    return pl.BlockSpec(memory_space=pltpu.VMEM)


def smem():
    return pl.BlockSpec(memory_space=pltpu.SMEM)


def fits(shape, kind):
    return math.prod(shape) * jnp.dtype(kind).itemsize <= SMALL


def near(value):
    return pltpu.with_memory_space_constraint(value, pltpu.VMEM) if fits(value.shape, value.dtype) else value


def call(kernel, outs, args, first=None, scratch=()):
    return pl.pallas_call(
        kernel,
        out_shape=[
            pltpu.VMEM(shape, kind) if inner and fits(shape, kind) else jax.ShapeDtypeStruct(shape, kind) for shape, kind, inner in outs
        ],
        in_specs=[first or vmem()] + [jax.tree.map(lambda _: vmem(), arg) for arg in args[1:]],
        out_specs=[vmem()] * len(outs),
        scratch_shapes=[pltpu.VMEM(shape, kind) for shape, kind in scratch],
    )(*args)


def exchange(value, axes):
    return lax.all_to_all(value, axes, 0, 0, tiled=True)


def on_device(embedding, w_left, w_right, w_in, w_out, w_head, dist_bias, offsets, valid_bins, target):
    rows, bands = lax.axis_size("rows"), lax.axis_size("band")
    devices = rows * bands
    bins, features = embedding.shape
    channels, hidden = w_in.shape
    tile = target.shape[-1]
    part = 2 * channels // bands
    blocks = channels // GROUP + 1
    noff = dist_bias.shape[1]
    quarter = features // bands
    flags = valid_bins.reshape(1, bins)

    (
        left,
        send,
        share,
        target_wide,
        w_both,
        parts,
        gain,
        logit_col,
        flag_col,
        head,
        bias,
        weights,
        w_in_near,
        w_out_near,
    ) = call(
        project_kernel,
        [
            ((channels, bins), BF, True),
            ((channels + GROUP, bins), BF, True),
            ((rows, bins, quarter), BF, True),
            ((tile, tile), F32, True),
            ((hidden, 2 * channels), BF, True),
            ((GROUP, 2 * GROUP, hidden), BF, True),
            ((hidden, 1), F32, True),
            ((tile, 1), F32, True),
            ((tile, 1), F32, True),
            ((channels, 1), F32, True),
            ((channels, 1), F32, True),
            ((2 * channels, quarter), BF, True),
            ((channels, hidden), BF, True),
            ((channels, hidden), BF, True),
        ],
        (
            offsets,
            embedding,
            w_left.T,
            w_right.T,
            flags,
            target.reshape(tile, tile),
            w_in,
            w_out.T,
            w_head.reshape(1, channels),
            dist_bias.T,
        ),
        smem(),
    )
    ahead = [send]
    for step in range(1, noff):
        ahead.append(lax.ppermute(send, "rows", [(source, source - step) for source in range(step, rows)]))
    emb_all = exchange(share, "rows")
    predicted, send = call(
        tile_kernel,
        [((tile, tile), BF, True), ((devices, part, tile), BF, True)],
        (
            offsets,
            near(left),
            [near(piece) for piece in ahead],
            near(target_wide),
            near(w_both),
            near(parts),
            near(gain),
            near(logit_col),
            near(flag_col),
            near(head),
            near(bias),
            near(w_in_near),
            near(w_out_near),
        ),
        smem(),
        [
            ((2, GROUP, hidden, tile), F32),
            ((2, GROUP, hidden, tile), F32),
            ((2, GROUP, channels, tile), BF),
            ((tile, tile), F32),
            ((tile, tile), F32),
            ((hidden, tile), F32),
            ((hidden, tile), F32),
            ((tile // GROUP, hidden, tile), F32),
        ],
    )
    send, emb_all = lax.optimization_barrier((send, emb_all))
    emb_far = lax.ppermute(emb_all, "band", [(source, source ^ HALVES) for source in range(bands)])
    partial = exchange(send, ("rows", "band"))
    (send,) = call(functools.partial(total_kernel, blocks), [((devices, part + GROUP, tile), BF, True)], (near(partial),))
    send, emb_far = lax.optimization_barrier((send, emb_far))
    complete = exchange(send, ("rows", "band"))
    (mine,) = call(
        share_kernel, [((2 * channels, features // HALVES), F32, True)], (near(complete), near(emb_all), near(emb_far))
    )
    other = lax.ppermute(mine, "band", [(source, source ^ 1) for source in range(bands)])
    predicted, grad_embedding, grad_in, grad_out, grad_head, grad_bias = call(
        finish_kernel,
        [
            ((tile, tile), BF, False),
            ((bins, features // bands), BF, False),
            ((channels, hidden), F32, False),
            ((channels, hidden), F32, False),
            ((1, channels), F32, False),
            (dist_bias.shape[::-1], F32, False),
        ],
        (near(complete), near(weights), near(head), near(predicted)),
    )
    grad_left, grad_right = call(arrange_kernel, [((channels, features), F32, False)] * 2, (near(mine), near(other)))
    return (
        predicted.reshape(target.shape),
        grad_embedding,
        grad_left.T,
        grad_right.T,
        grad_in,
        grad_out.T,
        grad_head.reshape(channels),
        grad_bias.T,
    )


def solution(mesh):
    placed = (
        P("rows", None),
        P(),
        P(),
        P(),
        P(),
        P(),
        P(),
        P("rows", "band"),
        P("rows"),
        P("rows", "band", None, None),
    )

    return jax.shard_map(
        on_device,
        mesh=mesh,
        in_specs=placed,
        out_specs=(P("rows", "band", None, None), P("rows", "band"), P(), P(), P(), P(), P(), P()),
        check_vma=False,
    )
```
